32 devices in a mesh: gy: 4 (over x, core), gz: 8 (over z, y).
Axes of the slice: x: 2, y: 2, z: 4, core: 2. Of those that a mesh axis runs over, the one named last changes fastest.
Arguments:
- velocity: float32 [3, 384, 6144], P(None, 'gy', 'gz'), may hold values from -250 to 250
- strain: bfloat16 [6, 384, 6144], P(None, 'gy', 'gz'), may hold values from -250 to 250
- cell_height: float32 [384], P('gy'), may hold values from 0.5 to 2
- stencil_reach: int32 [2, 384], P(None, 'gy'), may hold values from 1 to 8, as said below
Outputs:
- coefficient: float32 [384], P('gy')
The draws below stay inside these ranges and needn't reach their ends.
Inputs may be any that keep to these rules, and one draw needn't show every extreme that they name: `stencil_reach`: in every draw some plane reaches 8 planes on both sides; stencils are cut at the walls by the steps.
All inputs are finite; a program needn't handle non-finite values.
Results may differ from the reference program's by a relative error of at most 0.0003.
Values sent between devices are 32-bit elements; how exact they have to be, the bound alone decides.
A program may use at most 128 MiB of HBM per device.

```python
import math
import jax
import jax.numpy as jnp
from jax import lax

CZ = 96
NX = 8
HMAX = 8
NY = 384
NZ = 768


def column_scales(key):
    spread = math.log(10.0)
    stream_scale = jnp.exp(jax.random.uniform(jax.random.fold_in(key, 3), (NX,), jnp.float32, -0.5, 0.5) * spread)
    span_index = jnp.arange(NZ, dtype=jnp.int32)
    span_trend = jnp.exp(math.log(3.0) * (span_index.astype(jnp.float32) / NZ - 0.5))
    edge_cell = (span_index % CZ == 0) | (span_index % CZ == CZ - 1)
    edge_boost = jnp.where(edge_cell, 4.0, 1.0)
    span_scale = jnp.exp(jax.random.uniform(jax.random.fold_in(key, 5), (NZ,), jnp.float32, -0.5, 0.5) * spread) * span_trend * edge_boost
    return span_scale[:, None] * stream_scale[None, :]


def noise_field(key, array_shape):
    return jnp.clip(jax.random.normal(key, array_shape, jnp.float32), -5.0, 5.0)


def draw_velocity(key, part):
    scales = column_scales(jax.random.fold_in(key, 7))
    noise_data = noise_field(jax.random.fold_in(key, 11), (3, NY, NZ, NX))
    mean_flow = jax.random.uniform(jax.random.fold_in(key, 13), (NY,), jnp.float32, 0.5, 3.0)
    along_flow = mean_flow[:, None, None] + noise_data[0] * scales
    normal_part = (noise_data[1] - 0.5 * noise_data[0]) * scales
    across = noise_data[2] * scales
    stacked = jnp.stack([along_flow, normal_part, across])
    return jnp.clip(stacked, -249.0, 249.0).reshape(3, NY, NZ * NX).astype(jnp.float32)


def draw_strain(key, part):
    scales = column_scales(jax.random.fold_in(key, 7))
    noise_data = noise_field(jax.random.fold_in(key, 17), (6, NY, NZ, NX))
    shear_mean = jax.random.uniform(jax.random.fold_in(key, 19), (NY,), jnp.float32, 1.0, 3.0)
    lifted = noise_data.at[3].add(shear_mean[:, None, None])
    return jnp.clip(lifted * scales[None, None], -249.0, 249.0).reshape(6, NY, NZ * NX).astype(jnp.bfloat16)


def draw_stencil_reach(key, part):
    reach_draw = jax.random.randint(jax.random.fold_in(key, 23), (2, NY), 1, HMAX + 1, jnp.int32)
    return reach_draw.at[:, NY // 2].set(HMAX)


def levels(rng, extent, shards, least, top_value):
    gain = 1.0
    for dim, blocks in shards:
        steps = jax.random.uniform(jax.random.fold_in(jax.random.fold_in(rng, 6), dim), (blocks,), jnp.float32, least / len(shards), top_value / len(shards))
        gain = gain * jnp.repeat(jnp.exp(steps), extent[dim] // blocks).reshape((-1,) + (1,) * (len(extent) - 1 - dim))
    return gain


def setup_inputs(seed: int = 0) -> dict:
    keys = jax.random.split(jax.random.key(seed), 5)
    velocity = draw_velocity(jax.random.fold_in(keys[4], 71), 0)
    strain = draw_strain(jax.random.fold_in(keys[4], 71), 0)
    cell_height = jnp.clip(jnp.exp(math.log(2.0) - 1.3862944 * jax.random.uniform(keys[2], (NY,), jnp.float32) ** levels(keys[2], (NY,), ((0, 4),), -0.2, 0.2)), 0.5, 2.0)
    stencil_reach = draw_stencil_reach(jax.random.fold_in(keys[4], 71), 0)
    return dict(velocity=velocity, strain=strain, cell_height=cell_height, stencil_reach=stencil_reach)


LEAD_INDEX = (0, 1, 2, 0, 0, 1)
TAIL_INDEX = (0, 1, 2, 1, 2, 2)
TENSOR_WEIGHTS = (1.0, 1.0, 1.0, 2.0, 2.0, 2.0)

def strain_rate(tensor):
    squares = 2.0 * (tensor[0] * tensor[0] + tensor[1] * tensor[1] + tensor[2] * tensor[2])
    squares = squares + 4.0 * (tensor[3] * tensor[3] + tensor[4] * tensor[4] + tensor[5] * tensor[5])
    return jnp.sqrt(squares)

def axis_filter(field_data, axis_number):
    return 0.25 * jnp.roll(field_data, 1, axis_number) + 0.5 * field_data + 0.25 * jnp.roll(field_data, -1, axis_number)

def wall_coefficients(cell_height, stencil_reach):
    planes = jnp.arange(NY, dtype=jnp.int32)
    lowest = jnp.maximum(planes - stencil_reach[0], 0)
    highest = jnp.minimum(planes + stencil_reach[1], NY - 1)
    heights = jnp.pad(cell_height, (HMAX, HMAX))
    weight_terms = []
    for offset_plane in range(-HMAX, HMAX + 1):
        column = planes + offset_plane
        inside = (column >= lowest) & (column <= highest)
        weight_terms.append(jnp.where(inside, heights[HMAX + offset_plane:HMAX + offset_plane + NY], 0.0))
    weight_terms = jnp.stack(weight_terms)
    return weight_terms / lax.optimization_barrier(jnp.sum(weight_terms, axis=0, keepdims=True))

def test_filter(field_data, coefficients):
    field_data = axis_filter(field_data, 2)
    field_data = axis_filter(field_data, 1)
    padded = jnp.pad(field_data, ((HMAX, HMAX), (0, 0), (0, 0)))
    running_sum = jnp.zeros_like(field_data)
    for offset_plane in range(-HMAX, HMAX + 1):
        running_sum = running_sum + coefficients[offset_plane + HMAX][:, None, None] * padded[offset_plane + HMAX:offset_plane + HMAX + NY]
    return running_sum

def reference(velocity, strain, cell_height, stencil_reach):
    velocity = velocity.reshape(3, NY, NZ, NX)
    tensor = strain.astype(jnp.float32).reshape(6, NY, NZ, NX)
    coefficients = wall_coefficients(cell_height, stencil_reach)
    magnitude = strain_rate(tensor)
    velocity_bar = [test_filter(velocity[component], coefficients) for component in range(3)]
    tensor_bar = [test_filter(tensor[component], coefficients) for component in range(6)]
    rate_bar = strain_rate(tensor_bar)
    numerator = jnp.zeros((NY,), velocity.dtype)
    denominator = jnp.zeros((NY,), velocity.dtype)
    for component in range(6):
        first_index = LEAD_INDEX[component]
        second_index = TAIL_INDEX[component]
        product_bar = test_filter(velocity[first_index] * velocity[second_index], coefficients)
        model_bar = test_filter(magnitude * tensor[component], coefficients)
        leonard = product_bar - velocity_bar[first_index] * velocity_bar[second_index]
        model_term = model_bar - 4.0 * rate_bar * tensor_bar[component]
        numerator = numerator + lax.optimization_barrier(jnp.sum(TENSOR_WEIGHTS[component] * leonard * model_term, axis=(1, 2)))
        denominator = denominator + lax.optimization_barrier(jnp.sum(TENSOR_WEIGHTS[component] * model_term * model_term, axis=(1, 2)))
    cell_count = NZ * NX
    return numerator / cell_count / (denominator / cell_count + 1e-06)
```

```python
import functools

import jax
import jax.numpy as jnp
from jax import lax
from jax.experimental import pallas as pl
from jax.experimental.pallas import tpu as pltpu
from jax.sharding import PartitionSpec as P

NX = 8
HMAX = 8
LANES = 128
ROWS = 16

LEAD_INDEX = (0, 1, 2, 0, 0, 1)
TAIL_INDEX = (0, 1, 2, 1, 2, 2)
TENSOR_WEIGHTS = (1.0, 1.0, 1.0, 2.0, 2.0, 2.0)
FIELDS = 21
PACKED_AT = (
    [(0, c) for c in range(3)]
    + [(1, 0), (1, 1), (1, 2), (1, 9), (1, 11), (1, 10)]
    + [(0, 3 + c) for c in range(6)]
    + [(1, 3 + c) for c in range(6)]
)
MESH = pl.DeviceIdType.MESH


def strain_rate(t):
    squares = 2.0 * (t[0] * t[0] + t[1] * t[1] + t[2] * t[2])
    return jnp.sqrt(squares + 4.0 * (t[3] * t[3] + t[4] * t[4] + t[5] * t[5]))


def lane_index(rows):
    return lax.broadcasted_iota(jnp.int32, (rows, LANES), 1)


def streamwise4(x):
    position = lane_index(x.shape[0]) % NX
    behind = jnp.where(
        position == 0, pltpu.roll(x, LANES + 1 - NX, 1), pltpu.roll(x, 1, 1)
    )
    ahead = jnp.where(
        position == NX - 1, pltpu.roll(x, NX - 1, 1), pltpu.roll(x, LANES - 1, 1)
    )
    return behind + ahead + (x + x)


def horizontal(window, parted):
    shape = (3 * LANES, 2 * LANES)
    source = lax.broadcasted_iota(jnp.int32, shape, 0)
    target = lax.broadcasted_iota(jnp.int32, shape, 1) + LANES // 2
    cells_apart = jnp.abs(source // NX - target // NX)
    along = (source - target) & (NX - 1)
    span = jnp.where(cells_apart == 0, 2.0, jnp.where(cells_apart == 1, 1.0, 0.0))
    stream = jnp.where(along == 0, 2.0, jnp.where((along == 1) | (along == NX - 1), 1.0, 0.0))
    both = span * stream
    if parted:
        both = jnp.where((source < 2 * LANES) == (target < 2 * LANES), both, 0.0)
    both = both.astype(jnp.bfloat16)
    window[0 : 3 * LANES, :] = both
    window[3 * LANES : 6 * LANES, :] = both


def halves(x):
    high = x.astype(jnp.bfloat16)
    return high, (x - high.astype(jnp.float32)).astype(jnp.bfloat16)


def kernel(
    n_y,
    n_z,
    vel_hbm,
    strain_hbm,
    height_hbm,
    reach_hbm,
    out,
    vel,
    strain,
    height,
    reach,
    pieces,
    wall,
    window,
    window_parted,
    packed_pieces,
    packed_out,
    filt,
    halo_u,
    halo_s,
    send_s,
    strips,
    halo_strips,
    heights,
    halo_heights,
    acc,
    part,
    slots,
    send_sem,
    recv_sem,
    part_send,
    part_recv,
    load_sem,
    inside,
):
    planes, cells = vel.shape[1], vel.shape[2]
    all_planes = planes + 2 * HMAX
    loads = [
        pltpu.make_async_copy(strain_hbm, strain.at[:, 0:planes, :], load_sem.at[0]),
        pltpu.make_async_copy(vel_hbm, vel, load_sem.at[1]),
        pltpu.make_async_copy(height_hbm, height, load_sem.at[2]),
        pltpu.make_async_copy(reach_hbm, reach, load_sem.at[3]),
    ]
    for load in loads:
        load.start()
    tiles = cells // LANES
    my = lax.axis_index("gy")
    mz = lax.axis_index("gz")
    right = lax.rem(mz + 1, n_z)
    left = lax.rem(mz + n_z - 1, n_z)
    has_low = my > 0
    has_high = my < n_y - 1
    low = my - 1
    high = my + 1

    barrier = pltpu.get_barrier_semaphore()

    def greet(device):
        pl.semaphore_signal(barrier, inc=1, device_id=device, device_id_type=MESH)

    for step in range(1, n_z):
        greet({"gy": my, "gz": lax.rem(mz + step, n_z)})

    @pl.when(has_low)
    def _():
        for z in (mz, left, right):
            greet({"gy": low, "gz": z})

    @pl.when(has_high)
    def _():
        for z in (mz, left, right):
            greet({"gy": high, "gz": z})

    horizontal(window, False)
    horizontal(window_parted, True)
    for load in loads:
        load.wait()

    heights[...] = jnp.zeros_like(heights)
    heights[0:1, 0:planes] = height[...]
    heights[3:5, 0:planes] = reach[...].astype(jnp.float32)
    lane = lax.broadcasted_iota(jnp.int32, (planes, LANES), 1)
    sub = lax.broadcasted_iota(jnp.int32, (planes, LANES), 0)
    offset = my * planes
    column = offset + jnp.where(
        lane < planes, lane, jnp.where(lane < planes + HMAX, lane - planes - HMAX, lane - HMAX)
    )
    eye = lane == sub

    def upright(k):
        spread = jnp.where(eye, jnp.broadcast_to(heights[k : k + 1, :], (planes, LANES)), 0.0)
        return jnp.sum(spread, axis=1, keepdims=True).astype(jnp.int32)

    plane = offset + lax.broadcasted_iota(jnp.int32, (planes, 1), 0)
    lowest = jnp.maximum(plane - upright(3), 0)
    highest = jnp.minimum(plane + upright(4), n_y * planes - 1)
    allowed = (column >= lowest) & (column <= highest) & (lane < all_planes)
    inside[...] = jnp.where(allowed, 1.0, 0.0)

    for c in range(6):
        send_s[0, c] = strain[c, 0:ROWS, :].astype(jnp.float32)[0:HMAX]
        send_s[1, c] = strain[c, planes - ROWS : planes, :].astype(jnp.float32)[HMAX:ROWS]

    partners = (
        (n_z - 1)
        + 3 * has_low.astype(jnp.int32)
        + 3 * has_high.astype(jnp.int32)
    )
    pl.semaphore_wait(barrier, partners)

    def remote(src, dst, index, device):
        return pltpu.make_async_remote_copy(
            src_ref=src,
            dst_ref=dst,
            send_sem=send_sem.at[index],
            recv_sem=recv_sem.at[index],
            device_id=device,
            device_id_type=MESH,
        )

    top = slice(planes - HMAX, planes)
    under = slice(planes, planes + HMAX)
    over = slice(planes + HMAX, planes + 2 * HMAX)

    def to_high():
        here = {"gy": high, "gz": mz}
        return [
            remote(vel_hbm.at[:, top, :], halo_u.at[:, 0:HMAX, :], 0, here),
            remote(send_s.at[1], halo_s.at[:, 0:HMAX, :], 1, here),
            remote(height_hbm, halo_heights.at[0], 2, here),
            remote(strips.at[0, top, :], halo_strips.at[1, under, :], 3, {"gy": high, "gz": left}),
            remote(strips.at[1, top, :], halo_strips.at[0, under, :], 4, {"gy": high, "gz": right}),
        ]

    def to_low():
        here = {"gy": low, "gz": mz}
        return [
            remote(vel_hbm.at[:, 0:HMAX, :], halo_u.at[:, HMAX : 2 * HMAX, :], 5, here),
            remote(send_s.at[0], halo_s.at[:, HMAX : 2 * HMAX, :], 6, here),
            remote(height_hbm, halo_heights.at[1], 7, here),
            remote(strips.at[0, 0:HMAX, :], halo_strips.at[1, over, :], 8, {"gy": low, "gz": left}),
            remote(strips.at[1, 0:HMAX, :], halo_strips.at[0, over, :], 9, {"gy": low, "gz": right}),
        ]

    def to_sides():
        return [
            remote(strips.at[0], halo_strips.at[1, 0:planes, :], 10, {"gy": my, "gz": left}),
            remote(strips.at[1], halo_strips.at[0, 0:planes, :], 11, {"gy": my, "gz": right}),
        ]

    @pl.when(has_high)
    def _():
        for copy in to_high()[:3]:
            copy.start()

    @pl.when(has_low)
    def _():
        for copy in to_low()[:3]:
            copy.start()

    def pack(i, carry):
        rows = pl.ds(pl.multiple_of(i * ROWS, ROWS), ROWS)
        lane = lane_index(ROWS)
        first = jnp.zeros((ROWS, LANES), jnp.float32)
        last = first
        for g in range(9):
            def tile(start):
                if g < 3:
                    return vel[g, rows, start : start + LANES]
                return strain[g - 3, rows, start : start + LANES].astype(jnp.float32)

            here = (lane >= g * NX) & (lane < (g + 1) * NX)
            a = tile(0)
            b = tile(cells - LANES)
            first = jnp.where(here, pltpu.roll(a, g * NX, 1) if g else a, first)
            last = jnp.where(here, pltpu.roll(b, (g + 1) * NX, 1), last)
        strips[0, rows, :] = first
        strips[1, rows, :] = last
        return carry

    lax.fori_loop(0, planes // ROWS, pack, 0)

    def clear(side):
        span = slice(side * HMAX, (side + 1) * HMAX)
        halo_u[:, span, :] = jnp.zeros((3, HMAX, cells), jnp.float32)
        halo_s[:, span, :] = jnp.zeros((6, HMAX, cells), jnp.float32)
        halo_heights[side] = jnp.zeros(halo_heights.shape[1:], jnp.float32)
        start = planes + side * HMAX
        halo_strips[:, start : start + HMAX, :] = jnp.zeros((2, HMAX, LANES), jnp.float32)

    pl.when(jnp.logical_not(has_low))(lambda: clear(0))
    pl.when(jnp.logical_not(has_high))(lambda: clear(1))

    def form_block(load_u, load_s, start):
        rows = pl.ds(start, ROWS)
        low_rows = pl.ds(start + all_planes, ROWS)
        for t in range(tiles):
            lanes = slice(t * LANES, (t + 1) * LANES)

            def emit(f, x):
                hi, lo = halves(x)
                pieces[f, rows, lanes] = hi
                pieces[f, low_rows, lanes] = lo

            s = [load_s(c, lanes) for c in range(6)]
            rate = strain_rate(s)
            for c in range(6):
                emit(9 + c, rate * s[c])
            u = [load_u(c, lanes) for c in range(3)]
            for c in range(3):
                emit(c, u[c])
            for k in range(6):
                emit(3 + k, u[LEAD_INDEX[k]] * u[TAIL_INDEX[k]])

    def own_block(i, carry):
        start = pl.multiple_of(i * ROWS, ROWS)
        rows = pl.ds(start, ROWS)
        form_block(
            lambda c, lanes: vel[c, rows, lanes],
            lambda c, lanes: strain[c, rows, lanes].astype(jnp.float32),
            start,
        )
        return carry

    @pl.when(has_high)
    def _():
        for copy in to_high()[3:]:
            copy.start()

    @pl.when(has_low)
    def _():
        for copy in to_low()[3:]:
            copy.start()

    for copy in to_sides():
        copy.start()

    lax.fori_loop(0, planes // ROWS, own_block, 0)

    @pl.when(has_low)
    def _():
        for copy in to_high()[:3]:
            copy.wait_recv()

    @pl.when(has_high)
    def _():
        for copy in to_low()[:3]:
            copy.wait_recv()

    form_block(
        lambda c, lanes: halo_u[c, :, lanes],
        lambda c, lanes: halo_s[c, :, lanes],
        planes,
    )
    for c in range(6):
        strain[c, planes:all_planes, :] = halo_s[c].astype(jnp.bfloat16)

    heights[1:2, 0:planes] = halo_heights[0]
    heights[2:3, 0:planes] = halo_heights[1]
    own_row = heights[0:1, :]
    below_row = pltpu.roll(heights[1:2, :], LANES + planes - (planes - HMAX) - LANES, 1)
    above_row = pltpu.roll(heights[2:3, :], planes + HMAX, 1)
    lane_row = lax.broadcasted_iota(jnp.int32, (1, LANES), 1)
    row = jnp.where(
        lane_row < planes,
        own_row,
        jnp.where(lane_row < planes + HMAX, below_row, above_row),
    )
    weights = jnp.broadcast_to(row, (planes, LANES)) * inside[...]
    weights = weights / jnp.sum(weights, axis=1, keepdims=True) * (1.0 / 16.0)
    weights = weights[:, :all_planes]
    w_hi, w_lo = halves(weights)
    exact = jnp.concatenate([w_hi, w_lo], axis=0)
    matrix = jnp.concatenate(
        [
            jnp.concatenate([w_hi, w_hi], axis=1),
            jnp.concatenate([w_lo, jnp.zeros_like(w_lo)], axis=1),
        ],
        axis=0,
    )

    def band(weights, x):
        both = jnp.dot(weights, x, preferred_element_type=jnp.float32)
        return both[:planes] + both[planes:]


    def packed_edges():
        @pl.when(has_low)
        def _():
            for copy in to_high()[3:]:
                copy.wait_recv()

        @pl.when(has_high)
        def _():
            for copy in to_low()[3:]:
                copy.wait_recv()

        for copy in to_sides():
            copy.wait_recv()

        group = lane_index(all_planes) // NX
        scale = jnp.where(group < 3, 0.0, jnp.where(group < 6, 2.0, 4.0))
        for side in range(2):
            x = halo_strips[side]
            squares = x * x
            total = scale * squares
            for shift in (8, 16, 32, 64):
                total = total + pltpu.roll(total, shift, 1)
            rate = jnp.sqrt(total)
            one = pltpu.roll(x * pltpu.roll(x, NX, 1), 64, 1)
            two = pltpu.roll(x * pltpu.roll(x, 2 * NX, 1), 72, 1)
            second = jnp.where(
                group < 3,
                squares,
                jnp.where(group < 9, rate * x, jnp.where(group < 11, one, two)),
            )
            second = jnp.where(group < 12, second, 0.0)
            for k, y in enumerate((x, second)):
                hi, lo = halves(streamwise4(y))
                at = (2 * side + k) * LANES
                packed_pieces[0:all_planes, at : at + LANES] = hi
                packed_pieces[all_planes : 2 * all_planes, at : at + LANES] = lo
        packed_out[...] = band(matrix, packed_pieces[...])


    acc[...] = jnp.zeros_like(acc)
    width = 2 * LANES
    for f in range(FIELDS):
        rows = slice(f * planes, (f + 1) * planes)
        for start in range(0, cells, width):
            lanes = slice(start, start + width)
            if 9 <= f < 15:
                x = band(exact, strain[f - 9, :, lanes])
            else:
                x = band(matrix, pieces[f if f < 9 else f - 6, :, lanes])
            hi, lo = halves(x)
            wall[rows, lanes] = hi
            wall[rows, cells + start : cells + start + width] = lo

    for chunk in range(cells // width):
        last = chunk == cells // width - 1
        along = window_parted if last else window
        for f in range(0, FIELDS, 7):
            rows = slice(f * planes, (f + 7) * planes)
            columns = []
            for base in (0, cells):
                first = base + chunk * width
                if last:
                    columns.append(wall[rows, first : first + width])
                    columns.append(wall[rows, base : base + LANES])
                else:
                    columns.append(wall[rows, first : first + 3 * LANES])
            x = jnp.dot(
                jnp.concatenate(columns, axis=1),
                along[...],
                preferred_element_type=jnp.float32,
            )
            filt[chunk, f : f + 7] = x.reshape(7, planes, width)
        if last:
            packed_edges()
            half = LANES // 2
            for f in range(FIELDS):
                t, g = PACKED_AT[f]
                x = packed_out[:, t * LANES : (t + 1) * LANES]
                y = packed_out[:, (2 + t) * LANES : (3 + t) * LANES]
                x = pltpu.roll(x, (half - NX * g) % LANES, 1) if half != NX * g else x
                shift = (half - NX - NX * g) % LANES
                y = pltpu.roll(y, shift, 1) if shift else y
                x = jnp.where(
                    (lane >= half) & (lane < half + NX),
                    x,
                    jnp.where((lane >= half - NX) & (lane < half), y, 0.0),
                )
                filt[chunk, f, :, LANES:width] = filt[chunk, f, :, LANES:width] + x

        def contract(start):
            rows = slice(start, start + ROWS)
            numerator = jnp.zeros((ROWS, width), jnp.float32)
            denominator = jnp.zeros((ROWS, width), jnp.float32)
            tensor = [filt[chunk, 9 + c, rows, :] for c in range(6)]
            rate = 4.0 * strain_rate(tensor)
            for k in range(6):
                leonard = filt[chunk, 3 + k, rows, :] - filt[chunk, LEAD_INDEX[k], rows, :] * filt[chunk, TAIL_INDEX[k], rows, :]
                model = filt[chunk, 15 + k, rows, :] - rate * tensor[k]
                weighted = model if TENSOR_WEIGHTS[k] == 1.0 else TENSOR_WEIGHTS[k] * model
                numerator = numerator + leonard * weighted
                denominator = denominator + model * weighted
            for t in range(width // LANES):
                at = slice(t * LANES, (t + 1) * LANES)
                acc[rows, 0:LANES] = acc[rows, 0:LANES] + numerator[:, at]
                acc[rows, LANES : 2 * LANES] = acc[rows, LANES : 2 * LANES] + denominator[:, at]

        for start in range(0, planes, ROWS):
            contract(start)

    pick_row = lax.broadcasted_iota(jnp.int32, (8, 2 * LANES), 0)
    pick_lane = lax.broadcasted_iota(jnp.int32, (8, 2 * LANES), 1)
    pick = jnp.where(pick_row == pick_lane // LANES, 1.0, 0.0)
    part[...] = lax.dot_general(
        pick,
        acc[...],
        (((1,), (1,)), ((), ())),
        precision=lax.Precision.HIGHEST,
        preferred_element_type=jnp.float32,
    )
    slots[pl.ds(mz, 1)] = part[...][None]

    def share(step, peer, slot, sem):
        return pltpu.make_async_remote_copy(
            src_ref=part,
            dst_ref=slots.at[slot],
            send_sem=part_send.at[step],
            recv_sem=part_recv.at[sem],
            device_id={"gy": my, "gz": peer},
            device_id_type=MESH,
        )

    for step in range(1, n_z):
        peer = lax.rem(mz + step, n_z)
        share(step, peer, mz, step).start()
    for step in range(1, n_z):
        source = lax.rem(mz + n_z - step, n_z)
        share(step, source, source, step).wait_recv()
    total = jnp.zeros((8, LANES), jnp.float32)
    for k in range(n_z):
        total = total + slots[k]
    count = 1.0 * n_z * cells
    result = total[0:1] / count / (total[1:2] / count + 1e-6)
    out[...] = result[:, :planes]

    for step in range(1, n_z):
        peer = lax.rem(mz + step, n_z)
        share(step, peer, mz, step).wait_send()

    @pl.when(has_high)
    def _():
        for copy in to_high():
            copy.wait_send()

    @pl.when(has_low)
    def _():
        for copy in to_low():
            copy.wait_send()

    for copy in to_sides():
        copy.wait_send()


def local(velocity, strain, cell_height, stencil_reach):
    planes, cells = velocity.shape[1], velocity.shape[2]
    n_y = lax.axis_size("gy")
    n_z = lax.axis_size("gz")
    all_planes = planes + 2 * HMAX
    f32, bf16 = jnp.float32, jnp.bfloat16
    vmem = pl.BlockSpec(memory_space=pltpu.VMEM)
    result = pl.pallas_call(
        functools.partial(kernel, n_y, n_z),
        out_shape=jax.ShapeDtypeStruct((1, planes), f32),
        in_specs=[pl.BlockSpec(memory_space=pltpu.HBM)] * 4,
        out_specs=vmem,
        scratch_shapes=[
            pltpu.VMEM((3, planes, cells), f32),
            pltpu.VMEM((6, all_planes, cells), bf16),
            pltpu.VMEM((1, planes), f32),
            pltpu.VMEM((2, planes), jnp.int32),
            pltpu.VMEM((FIELDS - 6, 2 * all_planes, cells), bf16),
            pltpu.VMEM((FIELDS * planes, 2 * cells), bf16),
            pltpu.VMEM((6 * LANES, 2 * LANES), bf16),
            pltpu.VMEM((6 * LANES, 2 * LANES), bf16),
            pltpu.VMEM((2 * all_planes, 4 * LANES), bf16),
            pltpu.VMEM((planes, 4 * LANES), f32),
            pltpu.VMEM((cells // (2 * LANES), FIELDS, planes, 2 * LANES), f32),
            pltpu.VMEM((3, 2 * HMAX, cells), f32),
            pltpu.VMEM((6, 2 * HMAX, cells), f32),
            pltpu.VMEM((2, 6, HMAX, cells), f32),
            pltpu.VMEM((2, planes, LANES), f32),
            pltpu.VMEM((2, all_planes, LANES), f32),
            pltpu.VMEM((8, LANES), f32),
            pltpu.VMEM((2, 1, planes), f32),
            pltpu.VMEM((LANES, 2 * LANES), f32),
            pltpu.VMEM((8, LANES), f32),
            pltpu.VMEM((n_z, 8, LANES), f32),
            pltpu.SemaphoreType.DMA((12,)),
            pltpu.SemaphoreType.DMA((12,)),
            pltpu.SemaphoreType.DMA((n_z,)),
            pltpu.SemaphoreType.DMA((n_z,)),
            pltpu.SemaphoreType.DMA((4,)),
            pltpu.VMEM((planes, LANES), f32),
        ],
        compiler_params=pltpu.CompilerParams(
            collective_id=0, has_side_effects=True, vmem_limit_bytes=67043328
        ),
    )(velocity, strain, cell_height.reshape(1, planes), stencil_reach)
    return result.reshape(planes)


def solution(mesh):
    in_specs = (P(None, "gy", "gz"), P(None, "gy", "gz"), P("gy"), P(None, "gy"))
    return jax.shard_map(local, mesh=mesh, in_specs=in_specs, out_specs=P("gy"), check_vma=False)
```

```python
import functools

import jax
import jax.numpy as jnp
from jax import lax
from jax.experimental import pallas as pl
from jax.experimental.pallas import tpu as pltpu
from jax.sharding import PartitionSpec as P

NX = 8
HMAX = 8
LANES = 128
ROWS = 16

LEAD_INDEX = (0, 1, 2, 0, 0, 1)
TAIL_INDEX = (0, 1, 2, 1, 2, 2)
TENSOR_WEIGHTS = (1.0, 1.0, 1.0, 2.0, 2.0, 2.0)
FIELDS = 21
PACKED_AT = (
    [(0, 6), (0, 7), (2, 0)]
    + [(1, 6), (1, 7), (2, 1), (2, 5), (2, 6), (2, 7)]
    + [(0, c) for c in range(6)]
    + [(1, c) for c in range(6)]
)
MESH = pl.DeviceIdType.MESH


def strain_rate(t):
    squares = 2.0 * (t[0] * t[0] + t[1] * t[1] + t[2] * t[2])
    return jnp.sqrt(squares + 4.0 * (t[3] * t[3] + t[4] * t[4] + t[5] * t[5]))


def lane_index(rows):
    return lax.broadcasted_iota(jnp.int32, (rows, LANES), 1)


def streamwise4(x):
    position = lane_index(x.shape[0]) % NX
    behind = jnp.where(
        position == 0, pltpu.roll(x, LANES + 1 - NX, 1), pltpu.roll(x, 1, 1)
    )
    ahead = jnp.where(
        position == NX - 1, pltpu.roll(x, NX - 1, 1), pltpu.roll(x, LANES - 1, 1)
    )
    return behind + ahead + (x + x)


def horizontal(window, parted):
    shape = (3 * LANES, 2 * LANES)
    source = lax.broadcasted_iota(jnp.int32, shape, 0)
    target = lax.broadcasted_iota(jnp.int32, shape, 1) + LANES // 2
    cells_apart = jnp.abs(source // NX - target // NX)
    along = (source - target) & (NX - 1)
    span = jnp.where(cells_apart == 0, 2.0, jnp.where(cells_apart == 1, 1.0, 0.0))
    stream = jnp.where(along == 0, 2.0, jnp.where((along == 1) | (along == NX - 1), 1.0, 0.0))
    both = span * stream
    if parted:
        both = jnp.where((source < 2 * LANES) == (target < 2 * LANES), both, 0.0)
    both = both.astype(jnp.bfloat16)
    window[0 : 3 * LANES, :] = both
    window[3 * LANES : 6 * LANES, :] = both


def halves(x):
    high = x.astype(jnp.bfloat16)
    return high, (x - high.astype(jnp.float32)).astype(jnp.bfloat16)


def kernel(
    n_y,
    n_z,
    vel_hbm,
    strain_hbm,
    height_hbm,
    reach_hbm,
    out,
    vel,
    strain,
    height,
    reach,
    pieces,
    halo_pieces,
    wall,
    wall_rim,
    rim,
    window,
    window_parted,
    packed_pieces,
    packed_out,
    filt,
    halo_u,
    halo_s,
    halo_strain,
    send_s,
    strips,
    halo_strips,
    heights,
    halo_heights,
    upright_height,
    norm,
    acc,
    part,
    slots,
    send_sem,
    recv_sem,
    part_send,
    part_recv,
    load_sem,
    inside,
):
    planes, cells = vel.shape[1], vel.shape[2]
    all_planes = planes + 2 * HMAX
    inner = planes - 2 * HMAX
    bottom = slice(0, ROWS)
    middle = slice(ROWS, planes - ROWS)
    summit = slice(planes - ROWS, planes)
    loads = [
        pltpu.make_async_copy(height_hbm, height, load_sem.at[0]),
        pltpu.make_async_copy(reach_hbm, reach, load_sem.at[1]),
        pltpu.make_async_copy(strain_hbm.at[:, bottom, :], strain.at[:, bottom, :], load_sem.at[2]),
        pltpu.make_async_copy(strain_hbm.at[:, summit, :], strain.at[:, summit, :], load_sem.at[3]),
        pltpu.make_async_copy(vel_hbm, vel, load_sem.at[4]),
        pltpu.make_async_copy(strain_hbm.at[:, middle, :], strain.at[:, middle, :], load_sem.at[5]),
    ]
    for load in loads:
        load.start()
    tiles = cells // LANES
    my = lax.axis_index("gy")
    mz = lax.axis_index("gz")
    right = lax.rem(mz + 1, n_z)
    left = lax.rem(mz + n_z - 1, n_z)
    has_low = my > 0
    has_high = my < n_y - 1
    low = my - 1
    high = my + 1

    barrier = pltpu.get_barrier_semaphore()

    def greet(device):
        pl.semaphore_signal(barrier, inc=1, device_id=device, device_id_type=MESH)

    for step in range(1, n_z):
        greet({"gy": my, "gz": lax.rem(mz + step, n_z)})

    @pl.when(has_low)
    def _():
        for z in (mz, left, right):
            greet({"gy": low, "gz": z})

    @pl.when(has_high)
    def _():
        for z in (mz, left, right):
            greet({"gy": high, "gz": z})

    horizontal(window, False)
    horizontal(window_parted, True)

    for load in loads[:4]:
        load.wait()
    for c in range(6):
        send_s[0, c] = strain[c, 0:ROWS, :].astype(jnp.float32)[0:HMAX]
        send_s[1, c] = strain[c, planes - ROWS : planes, :].astype(jnp.float32)[HMAX:ROWS]

    heights[...] = jnp.zeros_like(heights)
    heights[0:1, 0:planes] = height[...]
    heights[3:5, 0:planes] = reach[...].astype(jnp.float32)
    lane = lax.broadcasted_iota(jnp.int32, (planes, LANES), 1)
    sub = lax.broadcasted_iota(jnp.int32, (planes, LANES), 0)
    own = jnp.where(sub < inner, sub + HMAX, jnp.where(sub < inner + HMAX, sub - inner, sub))
    offset = my * planes
    column = offset + jnp.where(
        lane < planes, lane, jnp.where(lane < planes + HMAX, lane - planes - HMAX, lane - HMAX)
    )

    def upright(k, at):
        rows = at.shape[0]
        spread = jnp.where(at, jnp.broadcast_to(heights[k : k + 1, :], (rows, LANES)), 0.0)
        return jnp.sum(spread, axis=1, keepdims=True)

    picked = lane == own
    plane = offset + own
    lowest = jnp.maximum(plane - upright(3, picked).astype(jnp.int32), 0)
    highest = jnp.minimum(plane + upright(4, picked).astype(jnp.int32), n_y * planes - 1)
    allowed = (column >= lowest) & (column <= highest) & (lane < all_planes)
    within = jnp.where(allowed, 1.0, 0.0)
    inside[...] = within
    own_row = heights[0:1, :]
    upright_height[0:planes, :] = jnp.broadcast_to(upright(0, lane == sub), (planes, LANES))
    weights = within * own_row
    total = jnp.sum(weights[0:inner], axis=1, keepdims=True)
    norm[0:inner, :] = jnp.broadcast_to((1.0 / 16.0) / total, (inner, LANES))
    mask = within.astype(jnp.bfloat16)
    mask_own = jnp.concatenate([mask[:, :planes]] * 2, axis=1)
    weights_own = jnp.concatenate(halves(weights[:, :planes]), axis=1)

    for load in loads[4:]:
        load.wait()

    def pack(i, carry):
        rows = pl.ds(pl.multiple_of(i * ROWS, ROWS), ROWS)
        lane = lane_index(ROWS)
        first = jnp.zeros((ROWS, LANES), jnp.float32)
        last = first
        for g in range(9):
            def tile(start):
                if g < 6:
                    return strain[g, rows, start : start + LANES].astype(jnp.float32)
                return vel[g - 6, rows, start : start + LANES]

            a = tile(0)
            b = tile(cells - LANES)
            to_first = 2 * g * NX if g < 8 else NX
            to_last = (2 * g + 1) * NX if g < 8 else 0
            a = pltpu.roll(a, to_first, 1) if to_first else a
            move = (to_last + NX) % LANES
            b = pltpu.roll(b, move, 1) if move else b
            first = jnp.where((lane >= to_first) & (lane < to_first + NX), a, first)
            last = jnp.where((lane >= to_last) & (lane < to_last + NX), b, last)
        strips[0, rows, :] = first
        strips[1, rows, :] = last
        return carry

    lax.fori_loop(0, planes // ROWS, pack, 0)

    def form_block(load_u, load_s, height_rows, into, hi_rows, lo_rows):
        h = upright_height[height_rows, :]
        for t in range(tiles):
            lanes = slice(t * LANES, (t + 1) * LANES)

            def emit(f, x):
                hi, lo = halves(x)
                into[f, hi_rows, lanes] = hi
                into[f, lo_rows, lanes] = lo

            s = [load_s(c, lanes) for c in range(6)]
            rate = h * strain_rate(s)
            for c in range(6):
                emit(9 + c, rate * s[c])
            u = [load_u(c, lanes) for c in range(3)]
            hu = [h * x for x in u]
            for c in range(3):
                emit(c, hu[c])
            for k in range(6):
                emit(3 + k, hu[LEAD_INDEX[k]] * u[TAIL_INDEX[k]])

    def own_block(i, carry):
        start = pl.multiple_of(i * ROWS, ROWS)
        rows = pl.ds(start, ROWS)
        form_block(
            lambda c, lanes: vel[c, rows, lanes],
            lambda c, lanes: strain[c, rows, lanes].astype(jnp.float32),
            rows,
            pieces,
            rows,
            pl.ds(start + planes, ROWS),
        )
        return carry

    partners = (
        (n_z - 1)
        + 3 * has_low.astype(jnp.int32)
        + 3 * has_high.astype(jnp.int32)
    )
    pl.semaphore_wait(barrier, partners)

    def remote(src, dst, index, device):
        return pltpu.make_async_remote_copy(
            src_ref=src,
            dst_ref=dst,
            send_sem=send_sem.at[index],
            recv_sem=recv_sem.at[index],
            device_id=device,
            device_id_type=MESH,
        )

    top = slice(planes - HMAX, planes)
    under = slice(planes, planes + HMAX)
    over = slice(planes + HMAX, planes + 2 * HMAX)

    def to_high():
        here = {"gy": high, "gz": mz}
        return [
            remote(height, halo_heights.at[0], 2, here),
            remote(vel_hbm.at[:, top, :], halo_u.at[:, 0:HMAX, :], 0, here),
            remote(send_s.at[1], halo_s.at[:, 0:HMAX, :], 1, here),
            remote(strips.at[0, top, :], halo_strips.at[1, under, :], 3, {"gy": high, "gz": left}),
            remote(strips.at[1, top, :], halo_strips.at[0, under, :], 4, {"gy": high, "gz": right}),
        ]

    def to_low():
        here = {"gy": low, "gz": mz}
        return [
            remote(height, halo_heights.at[1], 7, here),
            remote(vel_hbm.at[:, 0:HMAX, :], halo_u.at[:, HMAX : 2 * HMAX, :], 5, here),
            remote(send_s.at[0], halo_s.at[:, HMAX : 2 * HMAX, :], 6, here),
            remote(strips.at[0, 0:HMAX, :], halo_strips.at[1, over, :], 8, {"gy": low, "gz": left}),
            remote(strips.at[1, 0:HMAX, :], halo_strips.at[0, over, :], 9, {"gy": low, "gz": right}),
        ]

    def to_sides():
        return [
            remote(strips.at[0], halo_strips.at[1, 0:planes, :], 10, {"gy": my, "gz": left}),
            remote(strips.at[1], halo_strips.at[0, 0:planes, :], 11, {"gy": my, "gz": right}),
        ]

    @pl.when(has_high)
    def _():
        for copy in to_high():
            copy.start()

    @pl.when(has_low)
    def _():
        for copy in to_low():
            copy.start()

    for copy in to_sides():
        copy.start()

    def clear(side):
        span = slice(side * HMAX, (side + 1) * HMAX)
        halo_u[:, span, :] = jnp.zeros((3, HMAX, cells), jnp.float32)
        halo_s[:, span, :] = jnp.zeros((6, HMAX, cells), jnp.float32)
        halo_heights[side] = jnp.zeros(halo_heights.shape[1:], jnp.float32)
        start = planes + side * HMAX
        halo_strips[:, start : start + HMAX, :] = jnp.zeros((2, HMAX, LANES), jnp.float32)

    pl.when(jnp.logical_not(has_low))(lambda: clear(0))
    pl.when(jnp.logical_not(has_high))(lambda: clear(1))

    lax.fori_loop(0, planes // ROWS, own_block, 0)

    acc[...] = jnp.zeros_like(acc)
    width = 2 * LANES
    chunks = cells // width

    def put(ref, rows, start, x):
        hi, lo = halves(x)
        ref[rows, start : start + width] = hi
        ref[rows, cells + start : cells + start + width] = lo

    def band(weights, x):
        return jnp.dot(weights, x, preferred_element_type=jnp.float32)

    for f in range(FIELDS):
        for start in range(0, cells, width):
            lanes = slice(start, start + width)
            if 9 <= f < 15:
                s = strain[f - 9, :, lanes]
                x = band(weights_own, jnp.concatenate([s, s], axis=0))
            else:
                x = band(mask_own, pieces[f if f < 9 else f - 6, :, lanes])
            put(wall, slice(f * inner, (f + 1) * inner), start, x[:inner])
            rim[f, :, lanes] = x[inner:]

    def along(ref, rows, chunk):
        last = chunk == chunks - 1
        columns = []
        for base in (0, cells):
            first = base + chunk * width
            if last:
                columns.append(ref[rows, first : first + width])
                columns.append(ref[rows, base : base + LANES])
            else:
                columns.append(ref[rows, first : first + 3 * LANES])
        return jnp.dot(
            jnp.concatenate(columns, axis=1),
            (window_parted if last else window)[...],
            preferred_element_type=jnp.float32,
        )

    def contract(chunk, start, lanes):
        rows = slice(start, start + ROWS)
        q = norm[rows, :]

        def of(f):
            return filt[chunk, f, rows, lanes]

        tensor = [of(9 + c) for c in range(6)]
        rate = 4.0 * q * strain_rate(tensor)
        u = [of(c) for c in range(3)]
        qu = [q * x for x in u]
        sums = [[None, None], [None, None]]
        for k in range(6):
            leonard = of(3 + k) - qu[LEAD_INDEX[k]] * u[TAIL_INDEX[k]]
            model = of(15 + k) - rate * tensor[k]
            group = sums[0 if TENSOR_WEIGHTS[k] == 1.0 else 1]
            for at, term in enumerate((leonard * model, model * model)):
                group[at] = term if group[at] is None else group[at] + term
        for at in range(2):
            span = slice(at * LANES, (at + 1) * LANES)
            acc[rows, span] = acc[rows, span] + (sums[0][at] + 2.0 * sums[1][at])

    def contract_chunk(chunk, starts):
        for start in starts:
            for t in range(2):
                if chunk == chunks - 1 and t == 1:
                    continue
                contract(chunk, start, slice(t * LANES, (t + 1) * LANES))

    step_fields = 7
    for chunk in range(chunks):
        for f in range(0, FIELDS, step_fields):
            x = along(wall, slice(f * inner, (f + step_fields) * inner), chunk)
            filt[chunk, f : f + step_fields, 0:inner] = x.reshape(step_fields, inner, width)
        contract_chunk(chunk, range(0, inner, ROWS))

    @pl.when(has_low)
    def _():
        for copy in to_high()[:3]:
            copy.wait_recv()

    @pl.when(has_high)
    def _():
        for copy in to_low()[:3]:
            copy.wait_recv()

    heights[1:2, 0:planes] = halo_heights[0]
    heights[2:3, 0:planes] = halo_heights[1]
    below_row = pltpu.roll(heights[1:2, :], HMAX, 1)
    above_row = pltpu.roll(heights[2:3, :], planes + HMAX, 1)
    lane_row = lax.broadcasted_iota(jnp.int32, (1, LANES), 1)
    row = jnp.where(
        lane_row < planes,
        heights[0:1, :],
        jnp.where(lane_row < planes + HMAX, below_row, above_row),
    )
    heights[0:1, :] = row
    rim_lane = lax.broadcasted_iota(jnp.int32, (ROWS, LANES), 1)
    rim_sub = lax.broadcasted_iota(jnp.int32, (ROWS, LANES), 0)
    upright_height[planes:all_planes, :] = jnp.broadcast_to(
        upright(0, rim_lane == rim_sub + planes), (ROWS, LANES)
    )
    rim_inside = inside[inner:planes, :]
    rim_weights = rim_inside * row
    norm[inner:planes, :] = jnp.broadcast_to(
        (1.0 / 16.0) / jnp.sum(rim_weights, axis=1, keepdims=True), (ROWS, LANES)
    )
    rim_mask = jnp.concatenate([rim_inside.astype(jnp.bfloat16)[:, planes:all_planes]] * 2, axis=1)
    rim_weights = jnp.concatenate(halves(rim_weights[:, planes:all_planes]), axis=1)

    form_block(
        lambda c, lanes: halo_u[c, :, lanes],
        lambda c, lanes: halo_s[c, :, lanes],
        slice(planes, all_planes),
        halo_pieces,
        slice(0, ROWS),
        slice(ROWS, 2 * ROWS),
    )
    for c in range(6):
        halo_strain[c] = halo_s[c].astype(jnp.bfloat16)

    for f in range(FIELDS):
        for start in range(0, cells, width):
            lanes = slice(start, start + width)
            if 9 <= f < 15:
                s = halo_strain[f - 9, :, lanes]
                x = band(rim_weights, jnp.concatenate([s, s], axis=0))
            else:
                x = band(rim_mask, halo_pieces[f if f < 9 else f - 6, :, lanes])
            put(wall_rim, slice(f * ROWS, (f + 1) * ROWS), start, rim[f, :, lanes] + x)

    for chunk in range(chunks):
        x = along(wall_rim, slice(0, FIELDS * ROWS), chunk)
        filt[chunk, :, inner:planes] = x.reshape(FIELDS, ROWS, width)
        contract_chunk(chunk, [inner])

    @pl.when(has_low)
    def _():
        for copy in to_high()[3:]:
            copy.wait_recv()

    @pl.when(has_high)
    def _():
        for copy in to_low()[3:]:
            copy.wait_recv()

    for copy in to_sides():
        copy.wait_recv()

    strip_lane = lane_index(ROWS)
    group = strip_lane // (2 * NX)
    is_right = strip_lane % (2 * NX) < NX
    scale = jnp.where(group < 3, 2.0, jnp.where(group < 6, 4.0, 0.0))
    for start in range(0, all_planes, ROWS):
        rows = slice(start, start + ROWS)
        low_rows = slice(all_planes + start, all_planes + start + ROWS)
        h = upright_height[rows, :]
        from_left = halo_strips[0, rows, :]
        from_right = halo_strips[1, rows, :]
        a = jnp.where(is_right, from_right, from_left)
        b = jnp.where(is_right, pltpu.roll(from_right, LANES - NX, 1), pltpu.roll(from_left, NX, 1))
        b = jnp.where(group == 0, b, 0.0)
        ha = h * a
        hb = h * b
        total = scale * a * a
        for shift in (16, 32, 64):
            total = total + pltpu.roll(total, shift, 1)
        rate = jnp.sqrt(total)
        u2 = pltpu.roll(b, 6 * 16, 1) + pltpu.roll(b, 7 * 16, 1)
        mixed = pltpu.roll(ha * pltpu.roll(a, LANES - 16, 1), LANES - 16, 1)
        second = jnp.where(group < 6, rate * ha, ha * a)
        third = jnp.where(
            group < 5,
            hb + pltpu.roll(hb * b, 16, 1),
            jnp.where(group == 5, mixed, ha * u2),
        )
        for k, y in enumerate((ha, second, third)):
            hi, lo = halves(y)
            at = slice(k * LANES, (k + 1) * LANES)
            packed_pieces[rows, at] = hi
            packed_pieces[low_rows, at] = lo
    mask_all = inside[...].astype(jnp.bfloat16)[:, :all_planes]
    packed_out[...] = band(jnp.concatenate([mask_all, mask_all], axis=1), packed_pieces[...])

    half = LANES // 2
    joint = (strip_lane >= half - NX) & (strip_lane < half + NX)
    tail = slice(LANES, width)
    for start in range(0, planes, ROWS):
        rows = slice(start, start + ROWS)
        edge = [streamwise4(packed_out[rows, k * LANES : (k + 1) * LANES]) for k in range(3)]
        for f in range(FIELDS):
            t, g = PACKED_AT[f]
            shift = (half - NX - 2 * NX * g) % LANES
            x = pltpu.roll(edge[t], shift, 1) if shift else edge[t]
            filt[chunks - 1, f, rows, tail] = filt[chunks - 1, f, rows, tail] + jnp.where(joint, x, 0.0)
        contract(chunks - 1, start, tail)

    q = norm[...]
    scaled = jnp.concatenate([acc[:, 0:LANES] * (q * q), acc[:, LANES:width] * (q * q)], axis=1)
    pick_row = lax.broadcasted_iota(jnp.int32, (8, 2 * LANES), 0)
    pick_lane = lax.broadcasted_iota(jnp.int32, (8, 2 * LANES), 1)
    pick = jnp.where(pick_row == pick_lane // LANES, 1.0, 0.0)
    part[...] = jnp.zeros_like(part)
    part[:, 0:planes] = lax.dot_general(
        pick,
        scaled,
        (((1,), (1,)), ((), ())),
        precision=lax.Precision.HIGHEST,
        preferred_element_type=jnp.float32,
    )
    slots[pl.ds(mz, 1)] = part[...][None]

    def share(step, peer, slot, sem):
        return pltpu.make_async_remote_copy(
            src_ref=part,
            dst_ref=slots.at[slot],
            send_sem=part_send.at[step],
            recv_sem=part_recv.at[sem],
            device_id={"gy": my, "gz": peer},
            device_id_type=MESH,
        )

    for step in range(1, n_z):
        peer = lax.rem(mz + step, n_z)
        share(step, peer, mz, step).start()
    for step in range(1, n_z):
        source = lax.rem(mz + n_z - step, n_z)
        share(step, source, source, step).wait_recv()
    total = jnp.zeros((8, LANES), jnp.float32)
    for k in range(n_z):
        total = total + slots[k]
    count = 1.0 * n_z * cells
    result = total[0:1] / count / (total[1:2] / count + 1e-6)
    inner_row = pltpu.roll(result, HMAX, 1)
    low_row = pltpu.roll(result, LANES - inner, 1)
    result = jnp.where(
        lane_row < HMAX, low_row, jnp.where(lane_row < planes - HMAX, inner_row, result)
    )
    out[...] = result[:, :planes]

    for step in range(1, n_z):
        peer = lax.rem(mz + step, n_z)
        share(step, peer, mz, step).wait_send()

    @pl.when(has_high)
    def _():
        for copy in to_high():
            copy.wait_send()

    @pl.when(has_low)
    def _():
        for copy in to_low():
            copy.wait_send()

    for copy in to_sides():
        copy.wait_send()


def local(velocity, strain, cell_height, stencil_reach):
    planes, cells = velocity.shape[1], velocity.shape[2]
    n_y = lax.axis_size("gy")
    n_z = lax.axis_size("gz")
    all_planes = planes + 2 * HMAX
    inner = planes - 2 * HMAX
    f32, bf16 = jnp.float32, jnp.bfloat16
    vmem = pl.BlockSpec(memory_space=pltpu.VMEM)
    result = pl.pallas_call(
        functools.partial(kernel, n_y, n_z),
        out_shape=jax.ShapeDtypeStruct((1, planes), f32),
        in_specs=[pl.BlockSpec(memory_space=pltpu.HBM)] * 4,
        out_specs=vmem,
        scratch_shapes=[
            pltpu.VMEM((3, planes, cells), f32),
            pltpu.VMEM((6, planes, cells), bf16),
            pltpu.VMEM((1, planes), f32),
            pltpu.VMEM((2, planes), jnp.int32),
            pltpu.VMEM((FIELDS - 6, 2 * planes, cells), bf16),
            pltpu.VMEM((FIELDS - 6, 2 * ROWS, cells), bf16),
            pltpu.VMEM((FIELDS * inner, 2 * cells), bf16),
            pltpu.VMEM((FIELDS * ROWS, 2 * cells), bf16),
            pltpu.VMEM((FIELDS, ROWS, cells), f32),
            pltpu.VMEM((6 * LANES, 2 * LANES), bf16),
            pltpu.VMEM((6 * LANES, 2 * LANES), bf16),
            pltpu.VMEM((2 * all_planes, 3 * LANES), bf16),
            pltpu.VMEM((planes, 3 * LANES), f32),
            pltpu.VMEM((cells // (2 * LANES), FIELDS, planes, 2 * LANES), f32),
            pltpu.VMEM((3, 2 * HMAX, cells), f32),
            pltpu.VMEM((6, 2 * HMAX, cells), f32),
            pltpu.VMEM((6, 2 * HMAX, cells), bf16),
            pltpu.VMEM((2, 6, HMAX, cells), f32),
            pltpu.VMEM((2, planes, LANES), f32),
            pltpu.VMEM((2, all_planes, LANES), f32),
            pltpu.VMEM((8, LANES), f32),
            pltpu.VMEM((2, 1, planes), f32),
            pltpu.VMEM((all_planes, LANES), f32),
            pltpu.VMEM((planes, LANES), f32),
            pltpu.VMEM((planes, 2 * LANES), f32),
            pltpu.VMEM((8, LANES), f32),
            pltpu.VMEM((n_z, 8, LANES), f32),
            pltpu.SemaphoreType.DMA((12,)),
            pltpu.SemaphoreType.DMA((12,)),
            pltpu.SemaphoreType.DMA((n_z,)),
            pltpu.SemaphoreType.DMA((n_z,)),
            pltpu.SemaphoreType.DMA((6,)),
            pltpu.VMEM((planes, LANES), f32),
        ],
        compiler_params=pltpu.CompilerParams(
            collective_id=0, has_side_effects=True, vmem_limit_bytes=67043328
        ),
    )(velocity, strain, cell_height.reshape(1, planes), stencil_reach)
    return result.reshape(planes)


def solution(mesh):
    in_specs = (P(None, "gy", "gz"), P(None, "gy", "gz"), P("gy"), P(None, "gy"))
    return jax.shard_map(local, mesh=mesh, in_specs=in_specs, out_specs=P("gy"), check_vma=False)
```

```python
import functools

import jax
import jax.numpy as jnp
from jax import lax
from jax.experimental import pallas as pl
from jax.experimental.pallas import tpu as pltpu
from jax.sharding import PartitionSpec as P

NX = 8
HMAX = 8
LANES = 128
ROWS = 16

LEAD_INDEX = (0, 1, 2, 0, 0, 1)
TAIL_INDEX = (0, 1, 2, 1, 2, 2)
TENSOR_WEIGHTS = (1.0, 1.0, 1.0, 2.0, 2.0, 2.0)
FIELDS = 21
PACKED_AT = (
    [(0, 6), (0, 7), (2, 0)]
    + [(1, 6), (1, 7), (2, 1), (2, 5), (2, 6), (2, 7)]
    + [(0, c) for c in range(6)]
    + [(1, c) for c in range(6)]
)
MESH = pl.DeviceIdType.MESH


def strain_rate(t):
    squares = 2.0 * (t[0] * t[0] + t[1] * t[1] + t[2] * t[2])
    return jnp.sqrt(squares + 4.0 * (t[3] * t[3] + t[4] * t[4] + t[5] * t[5]))


def lane_index(rows):
    return lax.broadcasted_iota(jnp.int32, (rows, LANES), 1)


def streamwise4(x):
    position = lane_index(x.shape[0]) % NX
    behind = jnp.where(
        position == 0, pltpu.roll(x, LANES + 1 - NX, 1), pltpu.roll(x, 1, 1)
    )
    ahead = jnp.where(
        position == NX - 1, pltpu.roll(x, NX - 1, 1), pltpu.roll(x, LANES - 1, 1)
    )
    return behind + ahead + (x + x)


def horizontal(window, parted):
    shape = (3 * LANES, 2 * LANES)
    source = lax.broadcasted_iota(jnp.int32, shape, 0)
    target = lax.broadcasted_iota(jnp.int32, shape, 1) + LANES // 2
    cells_apart = jnp.abs(source // NX - target // NX)
    along = (source - target) & (NX - 1)
    span = jnp.where(cells_apart == 0, 2.0, jnp.where(cells_apart == 1, 1.0, 0.0))
    stream = jnp.where(along == 0, 2.0, jnp.where((along == 1) | (along == NX - 1), 1.0, 0.0))
    both = span * stream
    if parted:
        both = jnp.where((source < 2 * LANES) == (target < 2 * LANES), both, 0.0)
    both = both.astype(jnp.bfloat16)
    window[0 : 3 * LANES, :] = both
    window[3 * LANES : 6 * LANES, :] = both


def halves(x):
    high = x.astype(jnp.bfloat16)
    return high, (x - high.astype(jnp.float32)).astype(jnp.bfloat16)


def kernel(
    n_y,
    n_z,
    vel_hbm,
    strain_hbm,
    height_hbm,
    reach_hbm,
    out,
    vel,
    strain,
    height,
    reach,
    pieces,
    halo_pieces,
    wall,
    wall_rim,
    rim,
    window,
    window_parted,
    packed_pieces,
    rim_packed,
    packed_out,
    filt,
    halo_u,
    halo_s,
    send_s,
    strips,
    halo_strips,
    heights,
    halo_heights,
    upright_height,
    norm,
    acc,
    part,
    slots,
    send_sem,
    recv_sem,
    part_send,
    part_recv,
    load_sem,
    inside,
):
    planes, cells = vel.shape[1], vel.shape[2]
    all_planes = planes + 2 * HMAX
    inner = planes - 2 * HMAX
    bottom = slice(0, ROWS)
    middle = slice(ROWS, planes - ROWS)
    summit = slice(planes - ROWS, planes)
    loads = [
        pltpu.make_async_copy(height_hbm, height, load_sem.at[0]),
        pltpu.make_async_copy(reach_hbm, reach, load_sem.at[1]),
        pltpu.make_async_copy(strain_hbm.at[:, bottom, :], strain.at[:, bottom, :], load_sem.at[2]),
        pltpu.make_async_copy(strain_hbm.at[:, summit, :], strain.at[:, summit, :], load_sem.at[3]),
        pltpu.make_async_copy(vel_hbm, vel, load_sem.at[4]),
        pltpu.make_async_copy(strain_hbm.at[:, middle, :], strain.at[:, middle, :], load_sem.at[5]),
    ]
    for load in loads:
        load.start()
    tiles = cells // LANES
    my = lax.axis_index("gy")
    mz = lax.axis_index("gz")
    right = lax.rem(mz + 1, n_z)
    left = lax.rem(mz + n_z - 1, n_z)
    has_low = my > 0
    has_high = my < n_y - 1
    low = my - 1
    high = my + 1

    barrier = pltpu.get_barrier_semaphore()

    def greet(device):
        pl.semaphore_signal(barrier, inc=1, device_id=device, device_id_type=MESH)

    for step in range(1, n_z):
        greet({"gy": my, "gz": lax.rem(mz + step, n_z)})

    @pl.when(has_low)
    def _():
        for z in (mz, left, right):
            greet({"gy": low, "gz": z})

    @pl.when(has_high)
    def _():
        for z in (mz, left, right):
            greet({"gy": high, "gz": z})

    horizontal(window, False)
    horizontal(window_parted, True)

    for load in loads[:4]:
        load.wait()
    for c in range(6):
        send_s[0, c] = strain[c, 0:ROWS, :].astype(jnp.float32)[0:HMAX]
        send_s[1, c] = strain[c, planes - ROWS : planes, :].astype(jnp.float32)[HMAX:ROWS]

    heights[...] = jnp.zeros_like(heights)
    heights[0:1, 0:planes] = height[...]
    heights[3:5, 0:planes] = reach[...].astype(jnp.float32)
    lane = lax.broadcasted_iota(jnp.int32, (planes, LANES), 1)
    sub = lax.broadcasted_iota(jnp.int32, (planes, LANES), 0)
    own = jnp.where(sub < inner, sub + HMAX, jnp.where(sub < inner + HMAX, sub - inner, sub))
    offset = my * planes
    column = offset + jnp.where(
        lane < planes, lane, jnp.where(lane < planes + HMAX, lane - planes - HMAX, lane - HMAX)
    )

    def upright(k, at):
        rows = at.shape[0]
        spread = jnp.where(at, jnp.broadcast_to(heights[k : k + 1, :], (rows, LANES)), 0.0)
        return jnp.sum(spread, axis=1, keepdims=True)

    picked = lane == own
    plane = offset + own
    lowest = jnp.maximum(plane - upright(3, picked).astype(jnp.int32), 0)
    highest = jnp.minimum(plane + upright(4, picked).astype(jnp.int32), n_y * planes - 1)
    allowed = (column >= lowest) & (column <= highest) & (lane < all_planes)
    within = jnp.where(allowed, 1.0, 0.0)
    inside[...] = within
    own_row = heights[0:1, :]
    upright_height[0:planes, :] = jnp.broadcast_to(upright(0, lane == sub), (planes, LANES))
    weights = within * own_row
    total = jnp.sum(weights[0:inner], axis=1, keepdims=True)
    norm[0:inner, :] = jnp.broadcast_to((1.0 / 16.0) / total, (inner, LANES))
    mask = within.astype(jnp.bfloat16)
    mask_own = jnp.concatenate([mask[:, :planes]] * 2, axis=1)
    weights_own = jnp.concatenate(halves(weights[:, :planes]), axis=1)

    for load in loads[4:]:
        load.wait()

    def pack(i, carry):
        rows = pl.ds(pl.multiple_of(i * ROWS, ROWS), ROWS)
        lane = lane_index(ROWS)
        first = jnp.zeros((ROWS, LANES), jnp.float32)
        last = first
        for g in range(9):
            def tile(start):
                if g < 6:
                    return strain[g, rows, start : start + LANES].astype(jnp.float32)
                return vel[g - 6, rows, start : start + LANES]

            a = tile(0)
            b = tile(cells - LANES)
            to_first = 2 * g * NX if g < 8 else NX
            to_last = (2 * g + 1) * NX if g < 8 else 0
            a = pltpu.roll(a, to_first, 1) if to_first else a
            move = (to_last + NX) % LANES
            b = pltpu.roll(b, move, 1) if move else b
            first = jnp.where((lane >= to_first) & (lane < to_first + NX), a, first)
            last = jnp.where((lane >= to_last) & (lane < to_last + NX), b, last)
        strips[0, rows, :] = first
        strips[1, rows, :] = last
        return carry

    lax.fori_loop(0, planes // ROWS, pack, 0)

    def emit_to(into, hi_rows, lo_rows, lanes):
        def emit(f, x):
            hi, lo = halves(x)
            into[f, hi_rows, lanes] = hi
            into[f, lo_rows, lanes] = lo

        return emit

    def form_rates(load_s, height_rows, into, hi_rows, lo_rows):
        h = upright_height[height_rows, :]
        for t in range(tiles):
            lanes = slice(t * LANES, (t + 1) * LANES)
            emit = emit_to(into, hi_rows, lo_rows, lanes)
            s = [load_s(c, lanes) for c in range(6)]
            rate = h * strain_rate(s)
            for c in range(6):
                emit(9 + c, rate * s[c])

    def form_flow(load_u, height_rows, into, hi_rows, lo_rows):
        h = upright_height[height_rows, :]
        for t in range(tiles):
            lanes = slice(t * LANES, (t + 1) * LANES)
            emit = emit_to(into, hi_rows, lo_rows, lanes)
            u = [load_u(c, lanes) for c in range(3)]
            hu = [h * x for x in u]
            for c in range(3):
                emit(c, hu[c])
            for k in range(6):
                emit(3 + k, hu[LEAD_INDEX[k]] * u[TAIL_INDEX[k]])

    def own_block(i, carry):
        start = pl.multiple_of(i * ROWS, ROWS)
        rows = pl.ds(start, ROWS)
        places = (rows, pieces, rows, pl.ds(start + planes, ROWS))
        form_rates(lambda c, lanes: strain[c, rows, lanes].astype(jnp.float32), *places)
        form_flow(lambda c, lanes: vel[c, rows, lanes], *places)
        return carry

    blocks = planes // ROWS
    early = blocks - blocks // 3
    lax.fori_loop(0, early, own_block, 0)

    partners = (
        (n_z - 1)
        + 3 * has_low.astype(jnp.int32)
        + 3 * has_high.astype(jnp.int32)
    )
    pl.semaphore_wait(barrier, partners)

    def remote(src, dst, index, device):
        return pltpu.make_async_remote_copy(
            src_ref=src,
            dst_ref=dst,
            send_sem=send_sem.at[index],
            recv_sem=recv_sem.at[index],
            device_id=device,
            device_id_type=MESH,
        )

    top = slice(planes - HMAX, planes)
    under = slice(planes, planes + HMAX)
    over = slice(planes + HMAX, planes + 2 * HMAX)

    def to_high():
        here = {"gy": high, "gz": mz}
        return [
            remote(height, halo_heights.at[0], 2, here),
            remote(vel_hbm.at[:, top, :], halo_u.at[:, 0:HMAX, :], 0, here),
            remote(send_s.at[1], halo_s.at[:, 0:HMAX, :], 1, here),
            remote(strips.at[0, top, :], halo_strips.at[1, under, :], 3, {"gy": high, "gz": left}),
            remote(strips.at[1, top, :], halo_strips.at[0, under, :], 4, {"gy": high, "gz": right}),
        ]

    def to_low():
        here = {"gy": low, "gz": mz}
        return [
            remote(height, halo_heights.at[1], 7, here),
            remote(vel_hbm.at[:, 0:HMAX, :], halo_u.at[:, HMAX : 2 * HMAX, :], 5, here),
            remote(send_s.at[0], halo_s.at[:, HMAX : 2 * HMAX, :], 6, here),
            remote(strips.at[0, 0:HMAX, :], halo_strips.at[1, over, :], 8, {"gy": low, "gz": left}),
            remote(strips.at[1, 0:HMAX, :], halo_strips.at[0, over, :], 9, {"gy": low, "gz": right}),
        ]

    def to_sides():
        return [
            remote(strips.at[0], halo_strips.at[1, 0:planes, :], 10, {"gy": my, "gz": left}),
            remote(strips.at[1], halo_strips.at[0, 0:planes, :], 11, {"gy": my, "gz": right}),
        ]

    @pl.when(has_high)
    def _():
        for copy in to_high():
            copy.start()

    @pl.when(has_low)
    def _():
        for copy in to_low():
            copy.start()

    for copy in to_sides():
        copy.start()

    def clear(side):
        span = slice(side * HMAX, (side + 1) * HMAX)
        halo_u[:, span, :] = jnp.zeros((3, HMAX, cells), jnp.float32)
        halo_s[:, span, :] = jnp.zeros((6, HMAX, cells), jnp.float32)
        halo_heights[side] = jnp.zeros(halo_heights.shape[1:], jnp.float32)
        start = planes + side * HMAX
        halo_strips[:, start : start + HMAX, :] = jnp.zeros((2, HMAX, LANES), jnp.float32)

    pl.when(jnp.logical_not(has_low))(lambda: clear(0))
    pl.when(jnp.logical_not(has_high))(lambda: clear(1))

    lax.fori_loop(early, blocks, own_block, 0)

    acc[...] = jnp.zeros_like(acc)
    width = 2 * LANES
    chunks = cells // width

    def put(ref, rows, start, x):
        hi, lo = halves(x)
        ref[rows, start : start + width] = hi
        ref[rows, cells + start : cells + start + width] = lo

    def band(weights, x):
        return jnp.dot(weights, x, preferred_element_type=jnp.float32)

    for f in range(FIELDS):
        for start in range(0, cells, width):
            lanes = slice(start, start + width)
            if 9 <= f < 15:
                s = strain[f - 9, :, lanes]
                x = band(weights_own, jnp.concatenate([s, s], axis=0))
            else:
                x = band(mask_own, pieces[f if f < 9 else f - 6, :, lanes])
            put(wall, slice(f * inner, (f + 1) * inner), start, x[:inner])
            rim[f, :, lanes] = x[inner:]

    def along(ref, rows, chunk):
        last = chunk == chunks - 1
        columns = []
        for base in (0, cells):
            first = base + chunk * width
            if last:
                columns.append(ref[rows, first : first + width])
                columns.append(ref[rows, base : base + LANES])
            else:
                columns.append(ref[rows, first : first + 3 * LANES])
        return jnp.dot(
            jnp.concatenate(columns, axis=1),
            (window_parted if last else window)[...],
            preferred_element_type=jnp.float32,
        )

    def contract(chunk, start, t):
        rows = slice(start, start + 8)
        lanes = slice(t * LANES, (t + 1) * LANES)
        q = norm[rows, :]

        def of(f):
            return filt[chunk, f, rows, lanes]

        tensor = [of(9 + c) for c in range(6)]
        rate = 4.0 * q * strain_rate(tensor)
        u = [of(c) for c in range(3)]
        qu = [q * x for x in u]
        sums = [[None, None], [None, None]]
        for k in range(6):
            leonard = of(3 + k) - qu[LEAD_INDEX[k]] * u[TAIL_INDEX[k]]
            model = of(15 + k) - rate * tensor[k]
            group = sums[0 if TENSOR_WEIGHTS[k] == 1.0 else 1]
            for at, term in enumerate((leonard * model, model * model)):
                group[at] = term if group[at] is None else group[at] + term
        for at in range(2):
            span = slice(at * LANES, (at + 1) * LANES)
            acc[rows, span] = acc[rows, span] + (sums[0][at] + 2.0 * sums[1][at])

    def jobs(chunk, first, stop):
        parts = [0] if chunk == chunks - 1 else [0, 1]
        return [(chunk, start, t) for start in range(first, stop, 8) for t in parts]

    step_fields = 3
    pending = []
    for chunk in range(chunks):
        share_of = -(-len(pending) // (FIELDS // step_fields))
        for f in range(0, FIELDS, step_fields):
            x = along(wall, slice(f * inner, (f + step_fields) * inner), chunk)
            filt[chunk, f : f + step_fields, 0:inner] = x.reshape(step_fields, inner, width)
            for job in pending[:share_of]:
                contract(*job)
            pending = pending[share_of:]
        pending = jobs(chunk, 0, inner)

    for copy in to_sides():
        copy.wait_recv()

    strip_lane = lane_index(ROWS)
    group = strip_lane // (2 * NX)
    is_right = strip_lane % (2 * NX) < NX
    scale = jnp.where(group < 3, 2.0, jnp.where(group < 6, 4.0, 0.0))

    def form_strips(rows, into, hi_rows, lo_rows):
        h = upright_height[rows, :]
        from_left = halo_strips[0, rows, :]
        from_right = halo_strips[1, rows, :]
        a = jnp.where(is_right, from_right, from_left)
        b = jnp.where(is_right, pltpu.roll(from_right, LANES - NX, 1), pltpu.roll(from_left, NX, 1))
        b = jnp.where(group == 0, b, 0.0)
        ha = h * a
        hb = h * b
        total = scale * a * a
        for shift in (16, 32, 64):
            total = total + pltpu.roll(total, shift, 1)
        rate = jnp.sqrt(total)
        u2 = pltpu.roll(b, 6 * 16, 1) + pltpu.roll(b, 7 * 16, 1)
        mixed = pltpu.roll(ha * pltpu.roll(a, LANES - 16, 1), LANES - 16, 1)
        second = jnp.where(group < 6, rate * ha, ha * a)
        third = jnp.where(
            group < 5,
            hb + pltpu.roll(hb * b, 16, 1),
            jnp.where(group == 5, mixed, ha * u2),
        )
        for k, y in enumerate((ha, second, third)):
            hi, lo = halves(y)
            at = slice(k * LANES, (k + 1) * LANES)
            into[hi_rows, at] = hi
            into[lo_rows, at] = lo

    for start in range(0, planes, ROWS):
        rows = slice(start, start + ROWS)
        form_strips(rows, packed_pieces, rows, slice(planes + start, planes + start + ROWS))
    packed_out[...] = band(mask_own, packed_pieces[...])

    half = LANES // 2
    edge_lane = lane_index(8)
    joint = (edge_lane >= half - NX) & (edge_lane < half + NX)
    tail = slice(LANES, width)

    def add_edges(start):
        rows = slice(start, start + 8)
        edge = [streamwise4(packed_out[rows, k * LANES : (k + 1) * LANES]) for k in range(3)]
        for f in range(FIELDS):
            t, g = PACKED_AT[f]
            shift = (half - NX - 2 * NX * g) % LANES
            x = pltpu.roll(edge[t], shift, 1) if shift else edge[t]
            filt[chunks - 1, f, rows, tail] = filt[chunks - 1, f, rows, tail] + jnp.where(joint, x, 0.0)

    for job in pending:
        contract(*job)
    for start in range(0, inner, 8):
        add_edges(start)
        contract(chunks - 1, start, 1)

    def await_halo(which):
        @pl.when(has_low)
        def _():
            for copy in to_high()[which]:
                copy.wait_recv()

        @pl.when(has_high)
        def _():
            for copy in to_low()[which]:
                copy.wait_recv()

    await_halo(slice(0, 2))
    heights[1:2, 0:planes] = halo_heights[0]
    heights[2:3, 0:planes] = halo_heights[1]
    below_row = pltpu.roll(heights[1:2, :], HMAX, 1)
    above_row = pltpu.roll(heights[2:3, :], planes + HMAX, 1)
    lane_row = lax.broadcasted_iota(jnp.int32, (1, LANES), 1)
    row = jnp.where(
        lane_row < planes,
        heights[0:1, :],
        jnp.where(lane_row < planes + HMAX, below_row, above_row),
    )
    heights[0:1, :] = row
    rim_lane = lax.broadcasted_iota(jnp.int32, (ROWS, LANES), 1)
    rim_sub = lax.broadcasted_iota(jnp.int32, (ROWS, LANES), 0)
    upright_height[planes:all_planes, :] = jnp.broadcast_to(
        upright(0, rim_lane == rim_sub + planes), (ROWS, LANES)
    )
    rim_inside = inside[inner:planes, :]
    rim_weights = rim_inside * row
    norm[inner:planes, :] = jnp.broadcast_to(
        (1.0 / 16.0) / jnp.sum(rim_weights, axis=1, keepdims=True), (ROWS, LANES)
    )
    rim_mask = jnp.concatenate([rim_inside.astype(jnp.bfloat16)[:, planes:all_planes]] * 2, axis=1)
    rim_weights = jnp.concatenate(halves(rim_weights[:, planes:all_planes]), axis=1)

    rim_places = (slice(planes, all_planes), halo_pieces, slice(0, ROWS), slice(ROWS, 2 * ROWS))

    def rim_fields(first, stop):
        for f in range(first, stop):
            for start in range(0, cells, width):
                lanes = slice(start, start + width)
                if 9 <= f < 15:
                    s = halo_s[f - 9, :, lanes].astype(jnp.bfloat16)
                    x = band(rim_weights, jnp.concatenate([s, s], axis=0))
                else:
                    x = band(rim_mask, halo_pieces[f if f < 9 else f - 6, :, lanes])
                put(wall_rim, slice(f * ROWS, (f + 1) * ROWS), start, rim[f, :, lanes] + x)
        for chunk in range(chunks):
            x = along(wall_rim, slice(first * ROWS, stop * ROWS), chunk)
            filt[chunk, first:stop, inner:planes] = x.reshape(stop - first, ROWS, width)

    form_flow(lambda c, lanes: halo_u[c, :, lanes], *rim_places)
    rim_fields(0, 9)

    await_halo(slice(2, 3))
    form_rates(lambda c, lanes: halo_s[c, :, lanes], *rim_places)
    rim_fields(9, FIELDS)
    for chunk in range(chunks):
        for job in jobs(chunk, inner, planes):
            contract(*job)

    await_halo(slice(3, 5))
    form_strips(
        slice(planes, all_planes), rim_packed, slice(0, ROWS), slice(ROWS, 2 * ROWS)
    )
    packed_out[inner:planes, :] = packed_out[inner:planes, :] + band(rim_mask, rim_packed[...])
    for start in range(inner, planes, 8):
        add_edges(start)
        contract(chunks - 1, start, 1)

    q = norm[...]
    scaled = jnp.concatenate([acc[:, 0:LANES] * (q * q), acc[:, LANES:width] * (q * q)], axis=1)
    pick_row = lax.broadcasted_iota(jnp.int32, (2, 2 * LANES), 0)
    pick_lane = lax.broadcasted_iota(jnp.int32, (2, 2 * LANES), 1)
    pick = jnp.where(pick_row == pick_lane // LANES, 1.0, 0.0)
    part[...] = jnp.zeros_like(part)
    part[:, 0:planes] = lax.dot_general(
        pick,
        scaled,
        (((1,), (1,)), ((), ())),
        precision=lax.Precision.HIGHEST,
        preferred_element_type=jnp.float32,
    )
    slots[pl.ds(mz, 1)] = part[...][None]

    def share(step, peer, slot, sem):
        return pltpu.make_async_remote_copy(
            src_ref=part,
            dst_ref=slots.at[slot],
            send_sem=part_send.at[step],
            recv_sem=part_recv.at[sem],
            device_id={"gy": my, "gz": peer},
            device_id_type=MESH,
        )

    for step in range(1, n_z):
        peer = lax.rem(mz + step, n_z)
        share(step, peer, mz, step).start()
    for step in range(1, n_z):
        source = lax.rem(mz + n_z - step, n_z)
        share(step, source, source, step).wait_recv()
    total = jnp.zeros((2, LANES), jnp.float32)
    for k in range(n_z):
        total = total + slots[k]
    count = 1.0 * n_z * cells
    result = total[0:1] / count / (total[1:2] / count + 1e-6)
    inner_row = pltpu.roll(result, HMAX, 1)
    low_row = pltpu.roll(result, LANES - inner, 1)
    result = jnp.where(
        lane_row < HMAX, low_row, jnp.where(lane_row < planes - HMAX, inner_row, result)
    )
    out[...] = result[:, :planes]

    for step in range(1, n_z):
        peer = lax.rem(mz + step, n_z)
        share(step, peer, mz, step).wait_send()

    @pl.when(has_high)
    def _():
        for copy in to_high():
            copy.wait_send()

    @pl.when(has_low)
    def _():
        for copy in to_low():
            copy.wait_send()

    for copy in to_sides():
        copy.wait_send()


def local(velocity, strain, cell_height, stencil_reach):
    planes, cells = velocity.shape[1], velocity.shape[2]
    n_y = lax.axis_size("gy")
    n_z = lax.axis_size("gz")
    all_planes = planes + 2 * HMAX
    inner = planes - 2 * HMAX
    f32, bf16 = jnp.float32, jnp.bfloat16
    vmem = pl.BlockSpec(memory_space=pltpu.VMEM)
    result = pl.pallas_call(
        functools.partial(kernel, n_y, n_z),
        out_shape=jax.ShapeDtypeStruct((1, planes), f32),
        in_specs=[pl.BlockSpec(memory_space=pltpu.HBM)] * 4,
        out_specs=vmem,
        scratch_shapes=[
            pltpu.VMEM((3, planes, cells), f32),
            pltpu.VMEM((6, planes, cells), bf16),
            pltpu.VMEM((1, planes), f32),
            pltpu.VMEM((2, planes), jnp.int32),
            pltpu.VMEM((FIELDS - 6, 2 * planes, cells), bf16),
            pltpu.VMEM((FIELDS - 6, 2 * ROWS, cells), bf16),
            pltpu.VMEM((FIELDS * inner, 2 * cells), bf16),
            pltpu.VMEM((FIELDS * ROWS, 2 * cells), bf16),
            pltpu.VMEM((FIELDS, ROWS, cells), f32),
            pltpu.VMEM((6 * LANES, 2 * LANES), bf16),
            pltpu.VMEM((6 * LANES, 2 * LANES), bf16),
            pltpu.VMEM((2 * planes, 3 * LANES), bf16),
            pltpu.VMEM((2 * ROWS, 3 * LANES), bf16),
            pltpu.VMEM((planes, 3 * LANES), f32),
            pltpu.VMEM((cells // (2 * LANES), FIELDS, planes, 2 * LANES), f32),
            pltpu.VMEM((3, 2 * HMAX, cells), f32),
            pltpu.VMEM((6, 2 * HMAX, cells), f32),
            pltpu.VMEM((2, 6, HMAX, cells), f32),
            pltpu.VMEM((2, planes, LANES), f32),
            pltpu.VMEM((2, all_planes, LANES), f32),
            pltpu.VMEM((8, LANES), f32),
            pltpu.VMEM((2, 1, planes), f32),
            pltpu.VMEM((all_planes, LANES), f32),
            pltpu.VMEM((planes, LANES), f32),
            pltpu.VMEM((planes, 2 * LANES), f32),
            pltpu.VMEM((2, LANES), f32),
            pltpu.VMEM((n_z, 2, LANES), f32),
            pltpu.SemaphoreType.DMA((12,)),
            pltpu.SemaphoreType.DMA((12,)),
            pltpu.SemaphoreType.DMA((n_z,)),
            pltpu.SemaphoreType.DMA((n_z,)),
            pltpu.SemaphoreType.DMA((6,)),
            pltpu.VMEM((planes, LANES), f32),
        ],
        compiler_params=pltpu.CompilerParams(
            collective_id=0, has_side_effects=True, vmem_limit_bytes=67043328
        ),
    )(velocity, strain, cell_height.reshape(1, planes), stencil_reach)
    return result.reshape(planes)


def solution(mesh):
    in_specs = (P(None, "gy", "gz"), P(None, "gy", "gz"), P("gy"), P(None, "gy"))
    return jax.shard_map(local, mesh=mesh, in_specs=in_specs, out_specs=P("gy"), check_vma=False)
```

```python
import functools

import jax
import jax.numpy as jnp
from jax import lax
from jax.experimental import pallas as pl
from jax.experimental.pallas import tpu as pltpu
from jax.sharding import PartitionSpec as P

NX = 8
HMAX = 8
LANES = 128
ROWS = 16

LEAD_INDEX = (0, 1, 2, 0, 0, 1)
TAIL_INDEX = (0, 1, 2, 1, 2, 2)
TENSOR_WEIGHTS = (1.0, 1.0, 1.0, 2.0, 2.0, 2.0)
FIELDS = 21
PACKED_AT = (
    [(0, 6), (0, 7), (2, 0)]
    + [(1, 6), (1, 7), (2, 1), (2, 5), (2, 6), (2, 7)]
    + [(0, c) for c in range(6)]
    + [(1, c) for c in range(6)]
)
MESH = pl.DeviceIdType.MESH


def strain_rate(t):
    squares = 2.0 * (t[0] * t[0] + t[1] * t[1] + t[2] * t[2])
    return jnp.sqrt(squares + 4.0 * (t[3] * t[3] + t[4] * t[4] + t[5] * t[5]))


def lane_index(rows):
    return lax.broadcasted_iota(jnp.int32, (rows, LANES), 1)


def streamwise4(x):
    position = lane_index(x.shape[0]) % NX
    behind = jnp.where(
        position == 0, pltpu.roll(x, LANES + 1 - NX, 1), pltpu.roll(x, 1, 1)
    )
    ahead = jnp.where(
        position == NX - 1, pltpu.roll(x, NX - 1, 1), pltpu.roll(x, LANES - 1, 1)
    )
    return behind + ahead + (x + x)


def horizontal(window, parted):
    shape = (3 * LANES, 2 * LANES)
    source = lax.broadcasted_iota(jnp.int32, shape, 0)
    target = lax.broadcasted_iota(jnp.int32, shape, 1) + LANES // 2
    cells_apart = jnp.abs(source // NX - target // NX)
    along = (source - target) & (NX - 1)
    span = jnp.where(cells_apart == 0, 2.0, jnp.where(cells_apart == 1, 1.0, 0.0))
    stream = jnp.where(along == 0, 2.0, jnp.where((along == 1) | (along == NX - 1), 1.0, 0.0))
    both = span * stream
    if parted:
        both = jnp.where((source < 2 * LANES) == (target < 2 * LANES), both, 0.0)
    both = both.astype(jnp.bfloat16)
    window[0 : 3 * LANES, :] = both
    window[3 * LANES : 6 * LANES, :] = both


def halves(x):
    high = x.astype(jnp.bfloat16)
    return high, (x - high.astype(jnp.float32)).astype(jnp.bfloat16)


def kernel(
    n_y,
    n_z,
    vel_hbm,
    strain_hbm,
    height_hbm,
    reach_hbm,
    out,
    vel,
    strain,
    height,
    reach,
    pieces,
    halo_pieces,
    wall,
    wall_rim,
    rim,
    window,
    window_parted,
    packed_pieces,
    rim_packed,
    packed_out,
    filt,
    halo_u,
    halo_s,
    send_s,
    strips,
    halo_strips,
    heights,
    halo_heights,
    upright_height,
    norm,
    acc,
    part,
    slots,
    send_sem,
    recv_sem,
    part_send,
    part_recv,
    load_sem,
    known,
    inside,
):
    planes, cells = vel.shape[1], vel.shape[2]
    all_planes = planes + 2 * HMAX
    inner = planes - 2 * HMAX
    bottom = slice(0, ROWS)
    middle = slice(ROWS, planes - ROWS)
    summit = slice(planes - ROWS, planes)
    loads = [
        pltpu.make_async_copy(height_hbm, height, load_sem.at[0]),
        pltpu.make_async_copy(reach_hbm, reach, load_sem.at[1]),
        pltpu.make_async_copy(strain_hbm.at[:, bottom, :], strain.at[:, bottom, :], load_sem.at[2]),
        pltpu.make_async_copy(strain_hbm.at[:, summit, :], strain.at[:, summit, :], load_sem.at[3]),
        pltpu.make_async_copy(vel_hbm, vel, load_sem.at[4]),
        pltpu.make_async_copy(strain_hbm.at[:, middle, :], strain.at[:, middle, :], load_sem.at[5]),
    ]
    for load in loads:
        load.start()
    tiles = cells // LANES
    my = lax.axis_index("gy")
    mz = lax.axis_index("gz")
    right = lax.rem(mz + 1, n_z)
    left = lax.rem(mz + n_z - 1, n_z)
    has_low = my > 0
    has_high = my < n_y - 1
    low = my - 1
    high = my + 1

    barrier = pltpu.get_barrier_semaphore()

    def greet(device):
        pl.semaphore_signal(barrier, inc=1, device_id=device, device_id_type=MESH)

    greet({"gy": my, "gz": left})
    greet({"gy": my, "gz": right})
    pl.when(has_low)(lambda: greet({"gy": low, "gz": mz}))
    pl.when(has_high)(lambda: greet({"gy": high, "gz": mz}))

    horizontal(window, False)
    horizontal(window_parted, True)

    for load in loads[:4]:
        load.wait()
    for c in range(6):
        send_s[0, c] = strain[c, 0:ROWS, :].astype(jnp.float32)[0:HMAX]
        send_s[1, c] = strain[c, planes - ROWS : planes, :].astype(jnp.float32)[HMAX:ROWS]

    heights[...] = jnp.zeros_like(heights)
    heights[0:1, 0:planes] = height[...]
    heights[3:5, 0:planes] = reach[...].astype(jnp.float32)
    lane = lax.broadcasted_iota(jnp.int32, (planes, LANES), 1)
    sub = lax.broadcasted_iota(jnp.int32, (planes, LANES), 0)
    own = jnp.where(sub < inner, sub + HMAX, jnp.where(sub < inner + HMAX, sub - inner, sub))
    offset = my * planes
    column = offset + jnp.where(
        lane < planes, lane, jnp.where(lane < planes + HMAX, lane - planes - HMAX, lane - HMAX)
    )

    def upright(k, at):
        rows = at.shape[0]
        spread = jnp.where(at, jnp.broadcast_to(heights[k : k + 1, :], (rows, LANES)), 0.0)
        return jnp.sum(spread, axis=1, keepdims=True)

    picked = lane == own
    plane = offset + own
    lowest = jnp.maximum(plane - upright(3, picked).astype(jnp.int32), 0)
    highest = jnp.minimum(plane + upright(4, picked).astype(jnp.int32), n_y * planes - 1)
    allowed = (column >= lowest) & (column <= highest) & (lane < all_planes)
    within = jnp.where(allowed, 1.0, 0.0)
    inside[...] = within
    own_row = heights[0:1, :]
    upright_height[0:planes, :] = jnp.broadcast_to(upright(0, lane == sub), (planes, LANES))
    weights = within * own_row
    total = jnp.sum(weights[0:inner], axis=1, keepdims=True)
    norm[0:inner, :] = jnp.broadcast_to((1.0 / 16.0) / total, (inner, LANES))
    mask = within.astype(jnp.bfloat16)
    mask_own = jnp.concatenate([mask[:, :planes]] * 2, axis=1)
    weights_own = jnp.concatenate(halves(weights[:, :planes]), axis=1)

    for load in loads[4:]:
        load.wait()

    def pack(i, carry):
        rows = pl.ds(pl.multiple_of(i * ROWS, ROWS), ROWS)
        lane = lane_index(ROWS)
        first = jnp.zeros((ROWS, LANES), jnp.float32)
        last = first
        for g in range(9):
            def tile(start):
                if g < 6:
                    return strain[g, rows, start : start + LANES].astype(jnp.float32)
                return vel[g - 6, rows, start : start + LANES]

            a = tile(0)
            b = tile(cells - LANES)
            to_first = 2 * g * NX if g < 8 else NX
            to_last = (2 * g + 1) * NX if g < 8 else 0
            a = pltpu.roll(a, to_first, 1) if to_first else a
            move = (to_last + NX) % LANES
            b = pltpu.roll(b, move, 1) if move else b
            first = jnp.where((lane >= to_first) & (lane < to_first + NX), a, first)
            last = jnp.where((lane >= to_last) & (lane < to_last + NX), b, last)
        strips[0, rows, :] = first
        strips[1, rows, :] = last
        return carry

    lax.fori_loop(0, planes // ROWS, pack, 0)

    def emit_to(into, hi_rows, lo_rows, lanes):
        def emit(f, x):
            hi, lo = halves(x)
            into[f, hi_rows, lanes] = hi
            into[f, lo_rows, lanes] = lo

        return emit

    def form_rates(load_s, height_rows, into, hi_rows, lo_rows):
        h = upright_height[height_rows, :]
        for t in range(tiles):
            lanes = slice(t * LANES, (t + 1) * LANES)
            emit = emit_to(into, hi_rows, lo_rows, lanes)
            s = [load_s(c, lanes) for c in range(6)]
            rate = h * strain_rate(s)
            for c in range(6):
                emit(9 + c, rate * s[c])

    def form_flow(load_u, height_rows, into, hi_rows, lo_rows):
        h = upright_height[height_rows, :]
        for t in range(tiles):
            lanes = slice(t * LANES, (t + 1) * LANES)
            emit = emit_to(into, hi_rows, lo_rows, lanes)
            u = [load_u(c, lanes) for c in range(3)]
            hu = [h * x for x in u]
            for c in range(3):
                emit(c, hu[c])
            for k in range(6):
                emit(3 + k, hu[LEAD_INDEX[k]] * u[TAIL_INDEX[k]])

    def own_block(i, carry):
        start = pl.multiple_of(i * ROWS, ROWS)
        rows = pl.ds(start, ROWS)
        places = (rows, pieces, rows, pl.ds(start + planes, ROWS))
        form_rates(lambda c, lanes: strain[c, rows, lanes].astype(jnp.float32), *places)
        form_flow(lambda c, lanes: vel[c, rows, lanes], *places)
        return carry

    partners = 2 + has_low.astype(jnp.int32) + has_high.astype(jnp.int32)
    pl.semaphore_wait(barrier, partners)

    def tell(r):
        for z in (lax.rem(mz + 2**r, n_z), lax.rem(mz + n_z - 2**r, n_z)):
            pl.semaphore_signal(
                known.at[r], inc=1, device_id={"gy": my, "gz": z}, device_id_type=MESH
            )

    def hear(r):
        pl.semaphore_wait(known.at[r], 2)

    rounds = max((n_z // 2 - 1).bit_length(), 0)

    def remote(src, dst, index, device):
        return pltpu.make_async_remote_copy(
            src_ref=src,
            dst_ref=dst,
            send_sem=send_sem.at[index],
            recv_sem=recv_sem.at[index],
            device_id=device,
            device_id_type=MESH,
        )

    top = slice(planes - HMAX, planes)
    under = slice(planes, planes + HMAX)
    over = slice(planes + HMAX, planes + 2 * HMAX)

    def to_high():
        here = {"gy": high, "gz": mz}
        return [
            remote(height, halo_heights.at[0], 2, here),
            remote(vel_hbm.at[:, top, :], halo_u.at[:, 0:HMAX, :], 0, here),
            remote(send_s.at[1], halo_s.at[:, 0:HMAX, :], 1, here),
            remote(halo_strips.at[0, top, :], halo_strips.at[0, under, :], 3, here),
            remote(halo_strips.at[1, top, :], halo_strips.at[1, under, :], 4, here),
        ]

    def to_low():
        here = {"gy": low, "gz": mz}
        return [
            remote(height, halo_heights.at[1], 7, here),
            remote(vel_hbm.at[:, 0:HMAX, :], halo_u.at[:, HMAX : 2 * HMAX, :], 5, here),
            remote(send_s.at[0], halo_s.at[:, HMAX : 2 * HMAX, :], 6, here),
            remote(halo_strips.at[0, 0:HMAX, :], halo_strips.at[0, over, :], 8, here),
            remote(halo_strips.at[1, 0:HMAX, :], halo_strips.at[1, over, :], 9, here),
        ]

    def to_sides():
        return [
            remote(strips.at[0], halo_strips.at[1, 0:planes, :], 10, {"gy": my, "gz": left}),
            remote(strips.at[1], halo_strips.at[0, 0:planes, :], 11, {"gy": my, "gz": right}),
        ]

    def send_halo(which):
        @pl.when(has_high)
        def _():
            for copy in to_high()[which]:
                copy.start()

        @pl.when(has_low)
        def _():
            for copy in to_low()[which]:
                copy.start()

    send_halo(slice(0, 3))
    for copy in to_sides():
        copy.start()
    if rounds:
        tell(0)

    def clear(side):
        span = slice(side * HMAX, (side + 1) * HMAX)
        halo_u[:, span, :] = jnp.zeros((3, HMAX, cells), jnp.float32)
        halo_s[:, span, :] = jnp.zeros((6, HMAX, cells), jnp.float32)
        halo_heights[side] = jnp.zeros(halo_heights.shape[1:], jnp.float32)
        start = planes + side * HMAX
        halo_strips[:, start : start + HMAX, :] = jnp.zeros((2, HMAX, LANES), jnp.float32)

    pl.when(jnp.logical_not(has_low))(lambda: clear(0))
    pl.when(jnp.logical_not(has_high))(lambda: clear(1))

    lax.fori_loop(0, planes // ROWS, own_block, 0)

    acc[...] = jnp.zeros_like(acc)
    width = 2 * LANES
    chunks = cells // width

    def put(ref, rows, start, x):
        hi, lo = halves(x)
        ref[rows, start : start + width] = hi
        ref[rows, cells + start : cells + start + width] = lo

    def band(weights, x):
        return jnp.dot(weights, x, preferred_element_type=jnp.float32)

    for f in range(FIELDS):
        for start in range(0, cells, width):
            lanes = slice(start, start + width)
            if 9 <= f < 15:
                s = strain[f - 9, :, lanes]
                x = band(weights_own, jnp.concatenate([s, s], axis=0))
            else:
                x = band(mask_own, pieces[f if f < 9 else f - 6, :, lanes])
            put(wall, slice(f * inner, (f + 1) * inner), start, x[:inner])
            rim[f, :, lanes] = x[inner:]

    for r in range(1, rounds):
        hear(r - 1)
        tell(r)

    def along(ref, rows, chunk):
        last = chunk == chunks - 1
        columns = []
        for base in (0, cells):
            first = base + chunk * width
            if last:
                columns.append(ref[rows, first : first + width])
                columns.append(ref[rows, base : base + LANES])
            else:
                columns.append(ref[rows, first : first + 3 * LANES])
        return jnp.dot(
            jnp.concatenate(columns, axis=1),
            (window_parted if last else window)[...],
            preferred_element_type=jnp.float32,
        )

    def contract(chunk, start, t):
        rows = slice(start, start + 8)
        lanes = slice(t * LANES, (t + 1) * LANES)
        q = norm[rows, :]

        def of(f):
            return filt[chunk, f, rows, lanes]

        tensor = [of(9 + c) for c in range(6)]
        rate = 4.0 * q * strain_rate(tensor)
        u = [of(c) for c in range(3)]
        qu = [q * x for x in u]
        sums = [[None, None], [None, None]]
        for k in range(6):
            leonard = of(3 + k) - qu[LEAD_INDEX[k]] * u[TAIL_INDEX[k]]
            model = of(15 + k) - rate * tensor[k]
            group = sums[0 if TENSOR_WEIGHTS[k] == 1.0 else 1]
            for at, term in enumerate((leonard * model, model * model)):
                group[at] = term if group[at] is None else group[at] + term
        for at in range(2):
            span = slice(at * LANES, (at + 1) * LANES)
            acc[rows, span] = acc[rows, span] + (sums[0][at] + 2.0 * sums[1][at])

    def jobs(chunk, first, stop):
        parts = [0] if chunk == chunks - 1 else [0, 1]
        return [(chunk, start, t) for start in range(first, stop, 8) for t in parts]

    step_fields = 3
    pending = []
    for chunk in range(chunks):
        if chunk == chunks - 1:
            for copy in to_sides():
                copy.wait_recv()
            send_halo(slice(3, 5))
        share_of = -(-len(pending) // (FIELDS // step_fields))
        for f in range(0, FIELDS, step_fields):
            x = along(wall, slice(f * inner, (f + step_fields) * inner), chunk)
            filt[chunk, f : f + step_fields, 0:inner] = x.reshape(step_fields, inner, width)
            for job in pending[:share_of]:
                contract(*job)
            pending = pending[share_of:]
        pending = jobs(chunk, 0, inner)

    strip_lane = lane_index(ROWS)
    group = strip_lane // (2 * NX)
    is_right = strip_lane % (2 * NX) < NX
    scale = jnp.where(group < 3, 2.0, jnp.where(group < 6, 4.0, 0.0))

    def form_strips(rows, into, hi_rows, lo_rows):
        h = upright_height[rows, :]
        from_left = halo_strips[0, rows, :]
        from_right = halo_strips[1, rows, :]
        a = jnp.where(is_right, from_right, from_left)
        b = jnp.where(is_right, pltpu.roll(from_right, LANES - NX, 1), pltpu.roll(from_left, NX, 1))
        b = jnp.where(group == 0, b, 0.0)
        ha = h * a
        hb = h * b
        total = scale * a * a
        for shift in (16, 32, 64):
            total = total + pltpu.roll(total, shift, 1)
        rate = jnp.sqrt(total)
        u2 = pltpu.roll(b, 6 * 16, 1) + pltpu.roll(b, 7 * 16, 1)
        mixed = pltpu.roll(ha * pltpu.roll(a, LANES - 16, 1), LANES - 16, 1)
        second = jnp.where(group < 6, rate * ha, ha * a)
        third = jnp.where(
            group < 5,
            hb + pltpu.roll(hb * b, 16, 1),
            jnp.where(group == 5, mixed, ha * u2),
        )
        for k, y in enumerate((ha, second, third)):
            hi, lo = halves(y)
            at = slice(k * LANES, (k + 1) * LANES)
            into[hi_rows, at] = hi
            into[lo_rows, at] = lo

    for start in range(0, planes, ROWS):
        rows = slice(start, start + ROWS)
        form_strips(rows, packed_pieces, rows, slice(planes + start, planes + start + ROWS))
    packed_out[...] = band(mask_own, packed_pieces[...])

    half = LANES // 2
    edge_lane = lane_index(8)
    joint = (edge_lane >= half - NX) & (edge_lane < half + NX)
    tail = slice(LANES, width)

    def add_edges(start):
        rows = slice(start, start + 8)
        edge = [streamwise4(packed_out[rows, k * LANES : (k + 1) * LANES]) for k in range(3)]
        for f in range(FIELDS):
            t, g = PACKED_AT[f]
            shift = (half - NX - 2 * NX * g) % LANES
            x = pltpu.roll(edge[t], shift, 1) if shift else edge[t]
            filt[chunks - 1, f, rows, tail] = filt[chunks - 1, f, rows, tail] + jnp.where(joint, x, 0.0)

    for job in pending:
        contract(*job)
    for start in range(0, inner, 8):
        add_edges(start)
        contract(chunks - 1, start, 1)

    def await_halo(which):
        @pl.when(has_low)
        def _():
            for copy in to_high()[which]:
                copy.wait_recv()

        @pl.when(has_high)
        def _():
            for copy in to_low()[which]:
                copy.wait_recv()

    await_halo(slice(0, 2))
    heights[1:2, 0:planes] = halo_heights[0]
    heights[2:3, 0:planes] = halo_heights[1]
    below_row = pltpu.roll(heights[1:2, :], HMAX, 1)
    above_row = pltpu.roll(heights[2:3, :], planes + HMAX, 1)
    lane_row = lax.broadcasted_iota(jnp.int32, (1, LANES), 1)
    row = jnp.where(
        lane_row < planes,
        heights[0:1, :],
        jnp.where(lane_row < planes + HMAX, below_row, above_row),
    )
    heights[0:1, :] = row
    rim_lane = lax.broadcasted_iota(jnp.int32, (ROWS, LANES), 1)
    rim_sub = lax.broadcasted_iota(jnp.int32, (ROWS, LANES), 0)
    upright_height[planes:all_planes, :] = jnp.broadcast_to(
        upright(0, rim_lane == rim_sub + planes), (ROWS, LANES)
    )
    rim_inside = inside[inner:planes, :]
    rim_weights = rim_inside * row
    norm[inner:planes, :] = jnp.broadcast_to(
        (1.0 / 16.0) / jnp.sum(rim_weights, axis=1, keepdims=True), (ROWS, LANES)
    )
    rim_mask = jnp.concatenate([rim_inside.astype(jnp.bfloat16)[:, planes:all_planes]] * 2, axis=1)
    rim_weights = jnp.concatenate(halves(rim_weights[:, planes:all_planes]), axis=1)

    rim_places = (slice(planes, all_planes), halo_pieces, slice(0, ROWS), slice(ROWS, 2 * ROWS))

    def rim_fields(first, stop):
        for f in range(first, stop):
            for start in range(0, cells, width):
                lanes = slice(start, start + width)
                if 9 <= f < 15:
                    s = halo_s[f - 9, :, lanes].astype(jnp.bfloat16)
                    x = band(rim_weights, jnp.concatenate([s, s], axis=0))
                else:
                    x = band(rim_mask, halo_pieces[f if f < 9 else f - 6, :, lanes])
                put(wall_rim, slice(f * ROWS, (f + 1) * ROWS), start, rim[f, :, lanes] + x)
        for chunk in range(chunks):
            x = along(wall_rim, slice(first * ROWS, stop * ROWS), chunk)
            filt[chunk, first:stop, inner:planes] = x.reshape(stop - first, ROWS, width)

    form_flow(lambda c, lanes: halo_u[c, :, lanes], *rim_places)
    rim_fields(0, 9)

    await_halo(slice(2, 3))
    form_rates(lambda c, lanes: halo_s[c, :, lanes], *rim_places)
    rim_fields(9, FIELDS)
    for chunk in range(chunks):
        for job in jobs(chunk, inner, planes):
            contract(*job)

    await_halo(slice(3, 5))
    form_strips(
        slice(planes, all_planes), rim_packed, slice(0, ROWS), slice(ROWS, 2 * ROWS)
    )
    packed_out[inner:planes, :] = packed_out[inner:planes, :] + band(rim_mask, rim_packed[...])
    for start in range(inner, planes, 8):
        add_edges(start)
        contract(chunks - 1, start, 1)

    q = norm[...]
    scaled = jnp.concatenate([acc[:, 0:LANES] * (q * q), acc[:, LANES:width] * (q * q)], axis=1)
    pick_row = lax.broadcasted_iota(jnp.int32, (2, 2 * LANES), 0)
    pick_lane = lax.broadcasted_iota(jnp.int32, (2, 2 * LANES), 1)
    pick = jnp.where(pick_row == pick_lane // LANES, 1.0, 0.0)
    part[...] = jnp.zeros_like(part)
    part[:, 0:planes] = lax.dot_general(
        pick,
        scaled,
        (((1,), (1,)), ((), ())),
        precision=lax.Precision.HIGHEST,
        preferred_element_type=jnp.float32,
    )
    slots[pl.ds(mz, 1)] = part[...][None]

    def share(step, peer, slot, sem):
        return pltpu.make_async_remote_copy(
            src_ref=part,
            dst_ref=slots.at[slot],
            send_sem=part_send.at[step],
            recv_sem=part_recv.at[sem],
            device_id={"gy": my, "gz": peer},
            device_id_type=MESH,
        )

    if rounds:
        hear(rounds - 1)
    for step in range(1, n_z):
        peer = lax.rem(mz + step, n_z)
        share(step, peer, mz, step).start()
    for step in range(1, n_z):
        source = lax.rem(mz + n_z - step, n_z)
        share(step, source, source, step).wait_recv()
    total = jnp.zeros((2, LANES), jnp.float32)
    for k in range(n_z):
        total = total + slots[k]
    count = 1.0 * n_z * cells
    result = total[0:1] / count / (total[1:2] / count + 1e-6)
    inner_row = pltpu.roll(result, HMAX, 1)
    low_row = pltpu.roll(result, LANES - inner, 1)
    result = jnp.where(
        lane_row < HMAX, low_row, jnp.where(lane_row < planes - HMAX, inner_row, result)
    )
    out[...] = result[:, :planes]

    for step in range(1, n_z):
        peer = lax.rem(mz + step, n_z)
        share(step, peer, mz, step).wait_send()

    @pl.when(has_high)
    def _():
        for copy in to_high():
            copy.wait_send()

    @pl.when(has_low)
    def _():
        for copy in to_low():
            copy.wait_send()

    for copy in to_sides():
        copy.wait_send()


def local(velocity, strain, cell_height, stencil_reach):
    planes, cells = velocity.shape[1], velocity.shape[2]
    n_y = lax.axis_size("gy")
    n_z = lax.axis_size("gz")
    all_planes = planes + 2 * HMAX
    inner = planes - 2 * HMAX
    f32, bf16 = jnp.float32, jnp.bfloat16
    vmem = pl.BlockSpec(memory_space=pltpu.VMEM)
    result = pl.pallas_call(
        functools.partial(kernel, n_y, n_z),
        out_shape=jax.ShapeDtypeStruct((1, planes), f32),
        in_specs=[pl.BlockSpec(memory_space=pltpu.HBM)] * 4,
        out_specs=vmem,
        scratch_shapes=[
            pltpu.VMEM((3, planes, cells), f32),
            pltpu.VMEM((6, planes, cells), bf16),
            pltpu.VMEM((1, planes), f32),
            pltpu.VMEM((2, planes), jnp.int32),
            pltpu.VMEM((FIELDS - 6, 2 * planes, cells), bf16),
            pltpu.VMEM((FIELDS - 6, 2 * ROWS, cells), bf16),
            pltpu.VMEM((FIELDS * inner, 2 * cells), bf16),
            pltpu.VMEM((FIELDS * ROWS, 2 * cells), bf16),
            pltpu.VMEM((FIELDS, ROWS, cells), f32),
            pltpu.VMEM((6 * LANES, 2 * LANES), bf16),
            pltpu.VMEM((6 * LANES, 2 * LANES), bf16),
            pltpu.VMEM((2 * planes, 3 * LANES), bf16),
            pltpu.VMEM((2 * ROWS, 3 * LANES), bf16),
            pltpu.VMEM((planes, 3 * LANES), f32),
            pltpu.VMEM((cells // (2 * LANES), FIELDS, planes, 2 * LANES), f32),
            pltpu.VMEM((3, 2 * HMAX, cells), f32),
            pltpu.VMEM((6, 2 * HMAX, cells), f32),
            pltpu.VMEM((2, 6, HMAX, cells), f32),
            pltpu.VMEM((2, planes, LANES), f32),
            pltpu.VMEM((2, all_planes, LANES), f32),
            pltpu.VMEM((8, LANES), f32),
            pltpu.VMEM((2, 1, planes), f32),
            pltpu.VMEM((all_planes, LANES), f32),
            pltpu.VMEM((planes, LANES), f32),
            pltpu.VMEM((planes, 2 * LANES), f32),
            pltpu.VMEM((2, LANES), f32),
            pltpu.VMEM((n_z, 2, LANES), f32),
            pltpu.SemaphoreType.DMA((12,)),
            pltpu.SemaphoreType.DMA((12,)),
            pltpu.SemaphoreType.DMA((n_z,)),
            pltpu.SemaphoreType.DMA((n_z,)),
            pltpu.SemaphoreType.DMA((6,)),
            pltpu.SemaphoreType.REGULAR((max((n_z // 2 - 1).bit_length(), 1),)),
            pltpu.VMEM((planes, LANES), f32),
        ],
        compiler_params=pltpu.CompilerParams(
            collective_id=0, has_side_effects=True, vmem_limit_bytes=67043328
        ),
    )(velocity, strain, cell_height.reshape(1, planes), stencil_reach)
    return result.reshape(planes)


def solution(mesh):
    in_specs = (P(None, "gy", "gz"), P(None, "gy", "gz"), P("gy"), P(None, "gy"))
    return jax.shard_map(local, mesh=mesh, in_specs=in_specs, out_specs=P("gy"), check_vma=False)
```

```python
import functools

import jax
import jax.numpy as jnp
from jax import lax
from jax.experimental import pallas as pl
from jax.experimental.pallas import tpu as pltpu
from jax.sharding import PartitionSpec as P

NX = 8
HMAX = 8
LANES = 128
ROWS = 16

LEAD_INDEX = (0, 1, 2, 0, 0, 1)
TAIL_INDEX = (0, 1, 2, 1, 2, 2)
TENSOR_WEIGHTS = (1.0, 1.0, 1.0, 2.0, 2.0, 2.0)
FIELDS = 21
PACKED_AT = (
    [(0, 6), (0, 7), (2, 0)]
    + [(1, 6), (1, 7), (2, 1), (2, 5), (2, 6), (2, 7)]
    + [(0, c) for c in range(6)]
    + [(1, c) for c in range(6)]
)
MESH = pl.DeviceIdType.MESH


def strain_rate(t):
    squares = 2.0 * (t[0] * t[0] + t[1] * t[1] + t[2] * t[2])
    return jnp.sqrt(squares + 4.0 * (t[3] * t[3] + t[4] * t[4] + t[5] * t[5]))


def lane_index(rows):
    return lax.broadcasted_iota(jnp.int32, (rows, LANES), 1)


def streamwise4(x):
    position = lane_index(x.shape[0]) % NX
    behind = jnp.where(
        position == 0, pltpu.roll(x, LANES + 1 - NX, 1), pltpu.roll(x, 1, 1)
    )
    ahead = jnp.where(
        position == NX - 1, pltpu.roll(x, NX - 1, 1), pltpu.roll(x, LANES - 1, 1)
    )
    return behind + ahead + (x + x)


def horizontal(window, parted):
    shape = (3 * LANES, 2 * LANES)
    source = lax.broadcasted_iota(jnp.int32, shape, 0)
    target = lax.broadcasted_iota(jnp.int32, shape, 1) + LANES // 2
    cells_apart = jnp.abs(source // NX - target // NX)
    along = (source - target) & (NX - 1)
    span = jnp.where(cells_apart == 0, 2.0, jnp.where(cells_apart == 1, 1.0, 0.0))
    stream = jnp.where(along == 0, 2.0, jnp.where((along == 1) | (along == NX - 1), 1.0, 0.0))
    both = span * stream
    if parted:
        both = jnp.where((source < 2 * LANES) == (target < 2 * LANES), both, 0.0)
    both = both.astype(jnp.bfloat16)
    window[0 : 3 * LANES, :] = both
    window[3 * LANES : 6 * LANES, :] = both


def halves(x):
    high = x.astype(jnp.bfloat16)
    return high, (x - high.astype(jnp.float32)).astype(jnp.bfloat16)


def kernel(
    n_y,
    n_z,
    vel_hbm,
    strain_hbm,
    height_hbm,
    reach_hbm,
    out,
    vel,
    strain,
    height,
    reach,
    pieces,
    halo_pieces,
    wall,
    wall_rim,
    rim,
    window,
    window_parted,
    packed_pieces,
    rim_packed,
    packed_out,
    filt,
    halo_u,
    halo_s,
    send_s,
    strips,
    halo_strips,
    heights,
    halo_heights,
    upright_height,
    norm,
    acc,
    part,
    slots,
    send_sem,
    recv_sem,
    part_send,
    part_recv,
    load_sem,
    known,
    inside,
):
    planes, cells = vel.shape[1], vel.shape[2]
    all_planes = planes + 2 * HMAX
    inner = planes - 2 * HMAX
    ends = 2 * ROWS
    bottom = slice(0, ends)
    middle = slice(ends, planes - ROWS)
    summit = slice(planes - ROWS, planes)

    def load(src, dst, at):
        return pltpu.make_async_copy(src, dst, load_sem.at[at])

    loads = [
        load(height_hbm, height, 0),
        load(reach_hbm, reach, 1),
        load(strain_hbm.at[:, bottom, :], strain.at[:, bottom, :], 2),
        load(strain_hbm.at[:, summit, :], strain.at[:, summit, :], 3),
        load(vel_hbm.at[:, bottom, :], vel.at[:, bottom, :], 4),
        load(strain_hbm.at[:, middle, :], strain.at[:, middle, :], 5),
        load(vel_hbm.at[:, middle, :], vel.at[:, middle, :], 6),
        load(vel_hbm.at[:, summit, :], vel.at[:, summit, :], 7),
    ]
    for copy in loads:
        copy.start()
    tiles = cells // LANES
    my = lax.axis_index("gy")
    mz = lax.axis_index("gz")
    right = lax.rem(mz + 1, n_z)
    left = lax.rem(mz + n_z - 1, n_z)
    has_low = my > 0
    has_high = my < n_y - 1
    low = my - 1
    high = my + 1

    barrier = pltpu.get_barrier_semaphore()

    def greet(device):
        pl.semaphore_signal(barrier, inc=1, device_id=device, device_id_type=MESH)

    greet({"gy": my, "gz": left})
    greet({"gy": my, "gz": right})
    pl.when(has_low)(lambda: greet({"gy": low, "gz": mz}))
    pl.when(has_high)(lambda: greet({"gy": high, "gz": mz}))

    horizontal(window, False)
    horizontal(window_parted, True)

    for copy in loads[:4]:
        copy.wait()
    for c in range(6):
        send_s[0, c] = strain[c, 0:ROWS, :].astype(jnp.float32)[0:HMAX]
        send_s[1, c] = strain[c, planes - ROWS : planes, :].astype(jnp.float32)[HMAX:ROWS]

    heights[...] = jnp.zeros_like(heights)
    heights[0:1, 0:planes] = height[...]
    heights[3:5, 0:planes] = reach[...].astype(jnp.float32)
    lane = lax.broadcasted_iota(jnp.int32, (planes, LANES), 1)
    sub = lax.broadcasted_iota(jnp.int32, (planes, LANES), 0)
    own = jnp.where(sub < inner, sub + HMAX, jnp.where(sub < inner + HMAX, sub - inner, sub))
    offset = my * planes
    column = offset + jnp.where(
        lane < planes, lane, jnp.where(lane < planes + HMAX, lane - planes - HMAX, lane - HMAX)
    )

    def upright(k, at):
        rows = at.shape[0]
        spread = jnp.where(at, jnp.broadcast_to(heights[k : k + 1, :], (rows, LANES)), 0.0)
        return jnp.sum(spread, axis=1, keepdims=True)

    picked = lane == own
    plane = offset + own
    lowest = jnp.maximum(plane - upright(3, picked).astype(jnp.int32), 0)
    highest = jnp.minimum(plane + upright(4, picked).astype(jnp.int32), n_y * planes - 1)
    allowed = (column >= lowest) & (column <= highest) & (lane < all_planes)
    within = jnp.where(allowed, 1.0, 0.0)
    inside[...] = within
    own_row = heights[0:1, :]
    upright_height[0:planes, :] = jnp.broadcast_to(upright(0, lane == sub), (planes, LANES))
    weights = within * own_row
    total = jnp.sum(weights[0:inner], axis=1, keepdims=True)
    norm[0:inner, :] = jnp.broadcast_to((1.0 / 16.0) / total, (inner, LANES))
    mask = within.astype(jnp.bfloat16)
    mask_own = jnp.concatenate([mask[:, :planes]] * 2, axis=1)
    weights_own = jnp.concatenate(halves(weights[:, :planes]), axis=1)

    def pack(i, carry):
        rows = pl.ds(pl.multiple_of(i * ROWS, ROWS), ROWS)
        lane = lane_index(ROWS)
        first = jnp.zeros((ROWS, LANES), jnp.float32)
        last = first
        for g in range(9):
            def tile(start):
                if g < 6:
                    return strain[g, rows, start : start + LANES].astype(jnp.float32)
                return vel[g - 6, rows, start : start + LANES]

            a = tile(0)
            b = tile(cells - LANES)
            to_first = 2 * g * NX if g < 8 else NX
            to_last = (2 * g + 1) * NX if g < 8 else 0
            a = pltpu.roll(a, to_first, 1) if to_first else a
            move = (to_last + NX) % LANES
            b = pltpu.roll(b, move, 1) if move else b
            first = jnp.where((lane >= to_first) & (lane < to_first + NX), a, first)
            last = jnp.where((lane >= to_last) & (lane < to_last + NX), b, last)
        strips[0, rows, :] = first
        strips[1, rows, :] = last
        return carry


    def emit_to(into, hi_rows, lo_rows, lanes):
        def emit(f, x):
            hi, lo = halves(x)
            into[f, hi_rows, lanes] = hi
            into[f, lo_rows, lanes] = lo

        return emit

    def form_rates(load_s, height_rows, into, hi_rows, lo_rows):
        h = upright_height[height_rows, :]
        for t in range(tiles):
            lanes = slice(t * LANES, (t + 1) * LANES)
            emit = emit_to(into, hi_rows, lo_rows, lanes)
            s = [load_s(c, lanes) for c in range(6)]
            rate = h * strain_rate(s)
            for c in range(6):
                emit(9 + c, rate * s[c])

    def form_flow(load_u, height_rows, into, hi_rows, lo_rows):
        h = upright_height[height_rows, :]
        for t in range(tiles):
            lanes = slice(t * LANES, (t + 1) * LANES)
            emit = emit_to(into, hi_rows, lo_rows, lanes)
            u = [load_u(c, lanes) for c in range(3)]
            hu = [h * x for x in u]
            for c in range(3):
                emit(c, hu[c])
            for k in range(6):
                emit(3 + k, hu[LEAD_INDEX[k]] * u[TAIL_INDEX[k]])

    def own_block(i, carry):
        start = pl.multiple_of(i * ROWS, ROWS)
        rows = pl.ds(start, ROWS)
        places = (rows, pieces, rows, pl.ds(start + planes, ROWS))
        form_rates(lambda c, lanes: strain[c, rows, lanes].astype(jnp.float32), *places)
        form_flow(lambda c, lanes: vel[c, rows, lanes], *places)
        return carry

    loads[4].wait()
    lax.fori_loop(0, ends // ROWS, own_block, 0)
    for copy in loads[5:]:
        copy.wait()
    lax.fori_loop(0, planes // ROWS, pack, 0)

    partners = 2 + has_low.astype(jnp.int32) + has_high.astype(jnp.int32)
    pl.semaphore_wait(barrier, partners)

    def tell(r):
        for z in (lax.rem(mz + 2**r, n_z), lax.rem(mz + n_z - 2**r, n_z)):
            pl.semaphore_signal(
                known.at[r], inc=1, device_id={"gy": my, "gz": z}, device_id_type=MESH
            )

    def hear(r):
        pl.semaphore_wait(known.at[r], 2)

    rounds = max((n_z // 2 - 1).bit_length(), 0)

    def remote(src, dst, index, device):
        return pltpu.make_async_remote_copy(
            src_ref=src,
            dst_ref=dst,
            send_sem=send_sem.at[index],
            recv_sem=recv_sem.at[index],
            device_id=device,
            device_id_type=MESH,
        )

    top = slice(planes - HMAX, planes)
    under = slice(planes, planes + HMAX)
    over = slice(planes + HMAX, planes + 2 * HMAX)

    def to_high():
        here = {"gy": high, "gz": mz}
        return [
            remote(height, halo_heights.at[0], 2, here),
            remote(vel_hbm.at[:, top, :], halo_u.at[:, 0:HMAX, :], 0, here),
            remote(send_s.at[1], halo_s.at[:, 0:HMAX, :], 1, here),
            remote(strips.at[0, top, :], halo_strips.at[1, under, :], 3, {"gy": high, "gz": left}),
            remote(strips.at[1, top, :], halo_strips.at[0, under, :], 4, {"gy": high, "gz": right}),
        ]

    def to_low():
        here = {"gy": low, "gz": mz}
        return [
            remote(height, halo_heights.at[1], 7, here),
            remote(vel_hbm.at[:, 0:HMAX, :], halo_u.at[:, HMAX : 2 * HMAX, :], 5, here),
            remote(send_s.at[0], halo_s.at[:, HMAX : 2 * HMAX, :], 6, here),
            remote(strips.at[0, 0:HMAX, :], halo_strips.at[1, over, :], 8, {"gy": low, "gz": left}),
            remote(strips.at[1, 0:HMAX, :], halo_strips.at[0, over, :], 9, {"gy": low, "gz": right}),
        ]

    def to_sides():
        return [
            remote(strips.at[0], halo_strips.at[1, 0:planes, :], 10, {"gy": my, "gz": left}),
            remote(strips.at[1], halo_strips.at[0, 0:planes, :], 11, {"gy": my, "gz": right}),
        ]

    def send_halo(which):
        @pl.when(has_high)
        def _():
            for copy in to_high()[which]:
                copy.start()

        @pl.when(has_low)
        def _():
            for copy in to_low()[which]:
                copy.start()

    send_halo(slice(0, 3))
    for copy in to_sides():
        copy.start()
    if rounds:
        tell(0)

    def clear(side):
        span = slice(side * HMAX, (side + 1) * HMAX)
        halo_u[:, span, :] = jnp.zeros((3, HMAX, cells), jnp.float32)
        halo_s[:, span, :] = jnp.zeros((6, HMAX, cells), jnp.float32)
        halo_heights[side] = jnp.zeros(halo_heights.shape[1:], jnp.float32)
        start = planes + side * HMAX
        halo_strips[:, start : start + HMAX, :] = jnp.zeros((2, HMAX, LANES), jnp.float32)

    pl.when(jnp.logical_not(has_low))(lambda: clear(0))
    pl.when(jnp.logical_not(has_high))(lambda: clear(1))

    lax.fori_loop(ends // ROWS, planes // ROWS, own_block, 0)

    acc[...] = jnp.zeros_like(acc)
    width = 2 * LANES
    chunks = cells // width

    def put(ref, rows, start, x):
        hi, lo = halves(x)
        ref[rows, start : start + width] = hi
        ref[rows, cells + start : cells + start + width] = lo

    def band(weights, x):
        return jnp.dot(weights, x, preferred_element_type=jnp.float32)

    for f in range(FIELDS):
        for start in range(0, cells, width):
            lanes = slice(start, start + width)
            if 9 <= f < 15:
                s = strain[f - 9, :, lanes]
                x = band(weights_own, jnp.concatenate([s, s], axis=0))
            else:
                x = band(mask_own, pieces[f if f < 9 else f - 6, :, lanes])
            put(wall, slice(f * inner, (f + 1) * inner), start, x[:inner])
            rim[f, :, lanes] = x[inner:]

    def await_halo(which):
        @pl.when(has_low)
        def _():
            for copy in to_high()[which]:
                copy.wait_recv()

        @pl.when(has_high)
        def _():
            for copy in to_low()[which]:
                copy.wait_recv()

    await_halo(slice(0, 1))
    send_halo(slice(3, 5))
    for r in range(1, rounds):
        hear(r - 1)
        tell(r)

    def along(ref, rows, chunk):
        last = chunk == chunks - 1
        columns = []
        for base in (0, cells):
            first = base + chunk * width
            if last:
                columns.append(ref[rows, first : first + width])
                columns.append(ref[rows, base : base + LANES])
            else:
                columns.append(ref[rows, first : first + 3 * LANES])
        return jnp.dot(
            jnp.concatenate(columns, axis=1),
            (window_parted if last else window)[...],
            preferred_element_type=jnp.float32,
        )

    def contract(chunk, start, t):
        rows = slice(start, start + 8)
        lanes = slice(t * LANES, (t + 1) * LANES)
        q = norm[rows, :]

        def of(f):
            return filt[chunk, f, rows, lanes]

        tensor = [of(9 + c) for c in range(6)]
        rate = 4.0 * q * strain_rate(tensor)
        u = [of(c) for c in range(3)]
        qu = [q * x for x in u]
        sums = [[None, None], [None, None]]
        for k in range(6):
            leonard = of(3 + k) - qu[LEAD_INDEX[k]] * u[TAIL_INDEX[k]]
            model = of(15 + k) - rate * tensor[k]
            group = sums[0 if TENSOR_WEIGHTS[k] == 1.0 else 1]
            for at, term in enumerate((leonard * model, model * model)):
                group[at] = term if group[at] is None else group[at] + term
        for at in range(2):
            span = slice(at * LANES, (at + 1) * LANES)
            acc[rows, span] = acc[rows, span] + (sums[0][at] + 2.0 * sums[1][at])

    def jobs(chunk, first, stop):
        parts = [0] if chunk == chunks - 1 else [0, 1]
        return [(chunk, start, t) for start in range(first, stop, 8) for t in parts]

    step_fields = 3
    pending = []
    for chunk in range(chunks):
        share_of = -(-len(pending) // (FIELDS // step_fields))
        for f in range(0, FIELDS, step_fields):
            x = along(wall, slice(f * inner, (f + step_fields) * inner), chunk)
            filt[chunk, f : f + step_fields, 0:inner] = x.reshape(step_fields, inner, width)
            for job in pending[:share_of]:
                contract(*job)
            pending = pending[share_of:]
        pending = jobs(chunk, 0, inner)
    for job in pending:
        contract(*job)

    for copy in to_sides():
        copy.wait_recv()
    await_halo(slice(1, 3))

    strip_lane = lane_index(ROWS)
    group = strip_lane // (2 * NX)
    is_right = strip_lane % (2 * NX) < NX
    scale = jnp.where(group < 3, 2.0, jnp.where(group < 6, 4.0, 0.0))

    def form_strips(rows, into, hi_rows, lo_rows):
        h = upright_height[rows, :]
        from_left = halo_strips[0, rows, :]
        from_right = halo_strips[1, rows, :]
        a = jnp.where(is_right, from_right, from_left)
        b = jnp.where(is_right, pltpu.roll(from_right, LANES - NX, 1), pltpu.roll(from_left, NX, 1))
        b = jnp.where(group == 0, b, 0.0)
        ha = h * a
        hb = h * b
        total = scale * a * a
        for shift in (16, 32, 64):
            total = total + pltpu.roll(total, shift, 1)
        rate = jnp.sqrt(total)
        u2 = pltpu.roll(b, 6 * 16, 1) + pltpu.roll(b, 7 * 16, 1)
        mixed = pltpu.roll(ha * pltpu.roll(a, LANES - 16, 1), LANES - 16, 1)
        second = jnp.where(group < 6, rate * ha, ha * a)
        third = jnp.where(
            group < 5,
            hb + pltpu.roll(hb * b, 16, 1),
            jnp.where(group == 5, mixed, ha * u2),
        )
        for k, y in enumerate((ha, second, third)):
            hi, lo = halves(y)
            at = slice(k * LANES, (k + 1) * LANES)
            into[hi_rows, at] = hi
            into[lo_rows, at] = lo

    for start in range(0, planes, ROWS):
        rows = slice(start, start + ROWS)
        form_strips(rows, packed_pieces, rows, slice(planes + start, planes + start + ROWS))
    packed_out[...] = band(mask_own, packed_pieces[...])

    half = LANES // 2
    edge_lane = lane_index(8)
    joint = (edge_lane >= half - NX) & (edge_lane < half + NX)
    tail = slice(LANES, width)

    def add_edges(start):
        rows = slice(start, start + 8)
        edge = [streamwise4(packed_out[rows, k * LANES : (k + 1) * LANES]) for k in range(3)]
        for f in range(FIELDS):
            t, g = PACKED_AT[f]
            shift = (half - NX - 2 * NX * g) % LANES
            x = pltpu.roll(edge[t], shift, 1) if shift else edge[t]
            filt[chunks - 1, f, rows, tail] = filt[chunks - 1, f, rows, tail] + jnp.where(joint, x, 0.0)

    heights[1:2, 0:planes] = halo_heights[0]
    heights[2:3, 0:planes] = halo_heights[1]
    below_row = pltpu.roll(heights[1:2, :], HMAX, 1)
    above_row = pltpu.roll(heights[2:3, :], planes + HMAX, 1)
    lane_row = lax.broadcasted_iota(jnp.int32, (1, LANES), 1)
    row = jnp.where(
        lane_row < planes,
        heights[0:1, :],
        jnp.where(lane_row < planes + HMAX, below_row, above_row),
    )
    heights[0:1, :] = row
    rim_lane = lax.broadcasted_iota(jnp.int32, (ROWS, LANES), 1)
    rim_sub = lax.broadcasted_iota(jnp.int32, (ROWS, LANES), 0)
    upright_height[planes:all_planes, :] = jnp.broadcast_to(
        upright(0, rim_lane == rim_sub + planes), (ROWS, LANES)
    )
    rim_inside = inside[inner:planes, :]
    rim_weights = rim_inside * row
    norm[inner:planes, :] = jnp.broadcast_to(
        (1.0 / 16.0) / jnp.sum(rim_weights, axis=1, keepdims=True), (ROWS, LANES)
    )
    rim_mask = jnp.concatenate([rim_inside.astype(jnp.bfloat16)[:, planes:all_planes]] * 2, axis=1)
    rim_weights = jnp.concatenate(halves(rim_weights[:, planes:all_planes]), axis=1)

    rim_places = (slice(planes, all_planes), halo_pieces, slice(0, ROWS), slice(ROWS, 2 * ROWS))

    def rim_fields(first, stop):
        for f in range(first, stop):
            for start in range(0, cells, width):
                lanes = slice(start, start + width)
                if 9 <= f < 15:
                    s = halo_s[f - 9, :, lanes].astype(jnp.bfloat16)
                    x = band(rim_weights, jnp.concatenate([s, s], axis=0))
                else:
                    x = band(rim_mask, halo_pieces[f if f < 9 else f - 6, :, lanes])
                put(wall_rim, slice(f * ROWS, (f + 1) * ROWS), start, rim[f, :, lanes] + x)
        for chunk in range(chunks):
            x = along(wall_rim, slice(first * ROWS, stop * ROWS), chunk)
            filt[chunk, first:stop, inner:planes] = x.reshape(stop - first, ROWS, width)

    form_flow(lambda c, lanes: halo_u[c, :, lanes], *rim_places)
    form_rates(lambda c, lanes: halo_s[c, :, lanes], *rim_places)
    rim_fields(0, FIELDS)
    for start in range(0, inner, 8):
        add_edges(start)
        contract(chunks - 1, start, 1)
    for chunk in range(chunks):
        for job in jobs(chunk, inner, planes):
            contract(*job)

    await_halo(slice(3, 5))
    form_strips(
        slice(planes, all_planes), rim_packed, slice(0, ROWS), slice(ROWS, 2 * ROWS)
    )
    packed_out[inner:planes, :] = packed_out[inner:planes, :] + band(rim_mask, rim_packed[...])
    for start in range(inner, planes, 8):
        add_edges(start)
        contract(chunks - 1, start, 1)

    q = norm[...]
    scaled = jnp.concatenate([acc[:, 0:LANES] * (q * q), acc[:, LANES:width] * (q * q)], axis=1)
    pick_row = lax.broadcasted_iota(jnp.int32, (2, 2 * LANES), 0)
    pick_lane = lax.broadcasted_iota(jnp.int32, (2, 2 * LANES), 1)
    pick = jnp.where(pick_row == pick_lane // LANES, 1.0, 0.0)
    part[...] = jnp.zeros_like(part)
    part[:, 0:planes] = lax.dot_general(
        pick,
        scaled,
        (((1,), (1,)), ((), ())),
        precision=lax.Precision.HIGHEST,
        preferred_element_type=jnp.float32,
    )
    slots[pl.ds(mz, 1)] = part[...][None]

    def share(step, peer, slot, sem):
        return pltpu.make_async_remote_copy(
            src_ref=part,
            dst_ref=slots.at[slot],
            send_sem=part_send.at[step],
            recv_sem=part_recv.at[sem],
            device_id={"gy": my, "gz": peer},
            device_id_type=MESH,
        )

    if rounds:
        hear(rounds - 1)
    for step in range(1, n_z):
        peer = lax.rem(mz + step, n_z)
        share(step, peer, mz, step).start()
    for step in range(1, n_z):
        source = lax.rem(mz + n_z - step, n_z)
        share(step, source, source, step).wait_recv()
    total = jnp.zeros((2, LANES), jnp.float32)
    for k in range(n_z):
        total = total + slots[k]
    count = 1.0 * n_z * cells
    result = total[0:1] / count / (total[1:2] / count + 1e-6)
    inner_row = pltpu.roll(result, HMAX, 1)
    low_row = pltpu.roll(result, LANES - inner, 1)
    result = jnp.where(
        lane_row < HMAX, low_row, jnp.where(lane_row < planes - HMAX, inner_row, result)
    )
    out[...] = result[:, :planes]

    for step in range(1, n_z):
        peer = lax.rem(mz + step, n_z)
        share(step, peer, mz, step).wait_send()

    @pl.when(has_high)
    def _():
        for copy in to_high():
            copy.wait_send()

    @pl.when(has_low)
    def _():
        for copy in to_low():
            copy.wait_send()

    for copy in to_sides():
        copy.wait_send()


def local(velocity, strain, cell_height, stencil_reach):
    planes, cells = velocity.shape[1], velocity.shape[2]
    n_y = lax.axis_size("gy")
    n_z = lax.axis_size("gz")
    all_planes = planes + 2 * HMAX
    inner = planes - 2 * HMAX
    f32, bf16 = jnp.float32, jnp.bfloat16
    vmem = pl.BlockSpec(memory_space=pltpu.VMEM)
    result = pl.pallas_call(
        functools.partial(kernel, n_y, n_z),
        out_shape=jax.ShapeDtypeStruct((1, planes), f32),
        in_specs=[pl.BlockSpec(memory_space=pltpu.HBM)] * 4,
        out_specs=vmem,
        scratch_shapes=[
            pltpu.VMEM((3, planes, cells), f32),
            pltpu.VMEM((6, planes, cells), bf16),
            pltpu.VMEM((1, planes), f32),
            pltpu.VMEM((2, planes), jnp.int32),
            pltpu.VMEM((FIELDS - 6, 2 * planes, cells), bf16),
            pltpu.VMEM((FIELDS - 6, 2 * ROWS, cells), bf16),
            pltpu.VMEM((FIELDS * inner, 2 * cells), bf16),
            pltpu.VMEM((FIELDS * ROWS, 2 * cells), bf16),
            pltpu.VMEM((FIELDS, ROWS, cells), f32),
            pltpu.VMEM((6 * LANES, 2 * LANES), bf16),
            pltpu.VMEM((6 * LANES, 2 * LANES), bf16),
            pltpu.VMEM((2 * planes, 3 * LANES), bf16),
            pltpu.VMEM((2 * ROWS, 3 * LANES), bf16),
            pltpu.VMEM((planes, 3 * LANES), f32),
            pltpu.VMEM((cells // (2 * LANES), FIELDS, planes, 2 * LANES), f32),
            pltpu.VMEM((3, 2 * HMAX, cells), f32),
            pltpu.VMEM((6, 2 * HMAX, cells), f32),
            pltpu.VMEM((2, 6, HMAX, cells), f32),
            pltpu.VMEM((2, planes, LANES), f32),
            pltpu.VMEM((2, all_planes, LANES), f32),
            pltpu.VMEM((8, LANES), f32),
            pltpu.VMEM((2, 1, planes), f32),
            pltpu.VMEM((all_planes, LANES), f32),
            pltpu.VMEM((planes, LANES), f32),
            pltpu.VMEM((planes, 2 * LANES), f32),
            pltpu.VMEM((2, LANES), f32),
            pltpu.VMEM((n_z, 2, LANES), f32),
            pltpu.SemaphoreType.DMA((12,)),
            pltpu.SemaphoreType.DMA((12,)),
            pltpu.SemaphoreType.DMA((n_z,)),
            pltpu.SemaphoreType.DMA((n_z,)),
            pltpu.SemaphoreType.DMA((8,)),
            pltpu.SemaphoreType.REGULAR((max((n_z // 2 - 1).bit_length(), 1),)),
            pltpu.VMEM((planes, LANES), f32),
        ],
        compiler_params=pltpu.CompilerParams(
            collective_id=0, has_side_effects=True, vmem_limit_bytes=67043328 - 10490000
        ),
    )(velocity, strain, cell_height.reshape(1, planes), stencil_reach)
    return result.reshape(planes)


def solution(mesh):
    in_specs = (P(None, "gy", "gz"), P(None, "gy", "gz"), P("gy"), P(None, "gy"))
    return jax.shard_map(local, mesh=mesh, in_specs=in_specs, out_specs=P("gy"), check_vma=False)
```

```python
import functools

import jax
import jax.numpy as jnp
from jax import lax
from jax.experimental import pallas as pl
from jax.experimental.pallas import tpu as pltpu
from jax.sharding import PartitionSpec as P

NX = 8
HMAX = 8
LANES = 128
ROWS = 16

LEAD_INDEX = (0, 1, 2, 0, 0, 1)
TAIL_INDEX = (0, 1, 2, 1, 2, 2)
TENSOR_WEIGHTS = (1.0, 1.0, 1.0, 2.0, 2.0, 2.0)
FIELDS = 21
PACKED_AT = (
    [(0, 6), (0, 7), (2, 0)]
    + [(1, 6), (1, 7), (2, 1), (2, 5), (2, 6), (2, 7)]
    + [(0, c) for c in range(6)]
    + [(1, c) for c in range(6)]
)
MESH = pl.DeviceIdType.MESH


def strain_rate(t):
    squares = 2.0 * (t[0] * t[0] + t[1] * t[1] + t[2] * t[2])
    return jnp.sqrt(squares + 4.0 * (t[3] * t[3] + t[4] * t[4] + t[5] * t[5]))


def lane_index(rows):
    return lax.broadcasted_iota(jnp.int32, (rows, LANES), 1)


def streamwise4(x):
    position = lane_index(x.shape[0]) % NX
    behind = jnp.where(
        position == 0, pltpu.roll(x, LANES + 1 - NX, 1), pltpu.roll(x, 1, 1)
    )
    ahead = jnp.where(
        position == NX - 1, pltpu.roll(x, NX - 1, 1), pltpu.roll(x, LANES - 1, 1)
    )
    return behind + ahead + (x + x)


def horizontal(window, parted):
    shape = (3 * LANES, 2 * LANES)
    source = lax.broadcasted_iota(jnp.int32, shape, 0)
    target = lax.broadcasted_iota(jnp.int32, shape, 1) + LANES // 2
    cells_apart = jnp.abs(source // NX - target // NX)
    along = (source - target) & (NX - 1)
    span = jnp.where(cells_apart == 0, 2.0, jnp.where(cells_apart == 1, 1.0, 0.0))
    stream = jnp.where(along == 0, 2.0, jnp.where((along == 1) | (along == NX - 1), 1.0, 0.0))
    both = span * stream
    if parted:
        both = jnp.where((source < 2 * LANES) == (target < 2 * LANES), both, 0.0)
    both = both.astype(jnp.bfloat16)
    window[0 : 3 * LANES, :] = both
    window[3 * LANES : 6 * LANES, :] = both


def halves(x):
    high = x.astype(jnp.bfloat16)
    return high, (x - high.astype(jnp.float32)).astype(jnp.bfloat16)


def kernel(
    n_y,
    n_z,
    vel_hbm,
    strain_hbm,
    height_hbm,
    reach_hbm,
    out,
    vel,
    strain,
    height,
    reach,
    pieces,
    halo_pieces,
    wall,
    wall_rim,
    rim,
    window,
    window_parted,
    packed_pieces,
    rim_packed,
    packed_out,
    filt,
    halo_u,
    halo_s,
    send_s,
    strips,
    halo_strips,
    heights,
    halo_heights,
    upright_height,
    norm,
    acc,
    part,
    slots,
    send_sem,
    recv_sem,
    part_send,
    part_recv,
    load_sem,
    known,
    passed,
    inside,
):
    planes, cells = vel.shape[1], vel.shape[2]
    all_planes = planes + 2 * HMAX
    inner = planes - 2 * HMAX
    ends = 2 * ROWS
    bottom = slice(0, ends)
    middle = slice(ends, planes - ROWS)
    summit = slice(planes - ROWS, planes)

    def load(src, dst, at):
        return pltpu.make_async_copy(src, dst, load_sem.at[at])

    loads = [
        load(height_hbm, height, 0),
        load(reach_hbm, reach, 1),
        load(strain_hbm.at[:, bottom, :], strain.at[:, bottom, :], 2),
        load(strain_hbm.at[:, summit, :], strain.at[:, summit, :], 3),
        load(vel_hbm.at[:, bottom, :], vel.at[:, bottom, :], 4),
        load(strain_hbm.at[:, middle, :], strain.at[:, middle, :], 5),
        load(vel_hbm.at[:, middle, :], vel.at[:, middle, :], 6),
        load(vel_hbm.at[:, summit, :], vel.at[:, summit, :], 7),
    ]
    for copy in loads:
        copy.start()
    tiles = cells // LANES
    my = lax.axis_index("gy")
    mz = lax.axis_index("gz")
    right = lax.rem(mz + 1, n_z)
    left = lax.rem(mz + n_z - 1, n_z)
    has_low = my > 0
    has_high = my < n_y - 1
    low = my - 1
    high = my + 1

    barrier = pltpu.get_barrier_semaphore()

    def greet(device):
        pl.semaphore_signal(barrier, inc=1, device_id=device, device_id_type=MESH)

    greet({"gy": my, "gz": left})
    greet({"gy": my, "gz": right})
    pl.when(has_low)(lambda: greet({"gy": low, "gz": mz}))
    pl.when(has_high)(lambda: greet({"gy": high, "gz": mz}))

    horizontal(window, False)
    horizontal(window_parted, True)

    for copy in loads[:4]:
        copy.wait()
    for c in range(6):
        send_s[0, c] = strain[c, 0:ROWS, :].astype(jnp.float32)[0:HMAX]
        send_s[1, c] = strain[c, planes - ROWS : planes, :].astype(jnp.float32)[HMAX:ROWS]

    heights[...] = jnp.zeros_like(heights)
    heights[0:1, 0:planes] = height[...]
    heights[3:5, 0:planes] = reach[...].astype(jnp.float32)
    lane = lax.broadcasted_iota(jnp.int32, (planes, LANES), 1)
    sub = lax.broadcasted_iota(jnp.int32, (planes, LANES), 0)
    own = jnp.where(sub < inner, sub + HMAX, jnp.where(sub < inner + HMAX, sub - inner, sub))
    offset = my * planes
    column = offset + jnp.where(
        lane < planes, lane, jnp.where(lane < planes + HMAX, lane - planes - HMAX, lane - HMAX)
    )

    def upright(k, at):
        rows = at.shape[0]
        spread = jnp.where(at, jnp.broadcast_to(heights[k : k + 1, :], (rows, LANES)), 0.0)
        return jnp.sum(spread, axis=1, keepdims=True)

    picked = lane == own
    plane = offset + own
    lowest = jnp.maximum(plane - upright(3, picked).astype(jnp.int32), 0)
    highest = jnp.minimum(plane + upright(4, picked).astype(jnp.int32), n_y * planes - 1)
    allowed = (column >= lowest) & (column <= highest) & (lane < all_planes)
    within = jnp.where(allowed, 1.0, 0.0)
    inside[...] = within
    own_row = heights[0:1, :]
    upright_height[0:planes, :] = jnp.broadcast_to(upright(0, lane == sub), (planes, LANES))
    weights = within * own_row
    total = jnp.sum(weights[0:inner], axis=1, keepdims=True)
    norm[0:inner, :] = jnp.broadcast_to((1.0 / 16.0) / total, (inner, LANES))
    mask = within.astype(jnp.bfloat16)
    mask_own = jnp.concatenate([mask[:, :planes]] * 2, axis=1)
    weights_own = jnp.concatenate(halves(weights[:, :planes]), axis=1)

    def pack(i, carry):
        rows = pl.ds(pl.multiple_of(i * ROWS, ROWS), ROWS)
        lane = lane_index(ROWS)
        first = jnp.zeros((ROWS, LANES), jnp.float32)
        last = first
        for g in range(9):
            def tile(start):
                if g < 6:
                    return strain[g, rows, start : start + LANES].astype(jnp.float32)
                return vel[g - 6, rows, start : start + LANES]

            a = tile(0)
            b = tile(cells - LANES)
            to_first = 2 * g * NX if g < 8 else NX
            to_last = (2 * g + 1) * NX if g < 8 else 0
            a = pltpu.roll(a, to_first, 1) if to_first else a
            move = (to_last + NX) % LANES
            b = pltpu.roll(b, move, 1) if move else b
            first = jnp.where((lane >= to_first) & (lane < to_first + NX), a, first)
            last = jnp.where((lane >= to_last) & (lane < to_last + NX), b, last)
        strips[0, rows, :] = first
        strips[1, rows, :] = last
        return carry


    def emit_to(into, hi_rows, lo_rows, lanes):
        def emit(f, x):
            hi, lo = halves(x)
            into[f, hi_rows, lanes] = hi
            into[f, lo_rows, lanes] = lo

        return emit

    def form_rates(load_s, height_rows, into, hi_rows, lo_rows):
        h = upright_height[height_rows, :]
        for t in range(tiles):
            lanes = slice(t * LANES, (t + 1) * LANES)
            emit = emit_to(into, hi_rows, lo_rows, lanes)
            s = [load_s(c, lanes) for c in range(6)]
            rate = h * strain_rate(s)
            for c in range(6):
                emit(9 + c, rate * s[c])

    def form_flow(load_u, height_rows, into, hi_rows, lo_rows):
        h = upright_height[height_rows, :]
        for t in range(tiles):
            lanes = slice(t * LANES, (t + 1) * LANES)
            emit = emit_to(into, hi_rows, lo_rows, lanes)
            u = [load_u(c, lanes) for c in range(3)]
            hu = [h * x for x in u]
            for c in range(3):
                emit(c, hu[c])
            for k in range(6):
                emit(3 + k, hu[LEAD_INDEX[k]] * u[TAIL_INDEX[k]])

    def own_block(i, carry):
        start = pl.multiple_of(i * ROWS, ROWS)
        rows = pl.ds(start, ROWS)
        places = (rows, pieces, rows, pl.ds(start + planes, ROWS))
        form_rates(lambda c, lanes: strain[c, rows, lanes].astype(jnp.float32), *places)
        form_flow(lambda c, lanes: vel[c, rows, lanes], *places)
        return carry

    loads[4].wait()
    lax.fori_loop(0, ends // ROWS, own_block, 0)
    for copy in loads[5:]:
        copy.wait()
    lax.fori_loop(0, planes // ROWS, pack, 0)

    partners = 2 + has_low.astype(jnp.int32) + has_high.astype(jnp.int32)
    pl.semaphore_wait(barrier, partners)

    def tell(r):
        for z in (lax.rem(mz + 2**r, n_z), lax.rem(mz + n_z - 2**r, n_z)):
            pl.semaphore_signal(
                known.at[r], inc=1, device_id={"gy": my, "gz": z}, device_id_type=MESH
            )

    def hear(r):
        pl.semaphore_wait(known.at[r], 2)

    rounds = max((n_z // 2 - 1).bit_length(), 0)

    def remote(src, dst, index, device):
        return pltpu.make_async_remote_copy(
            src_ref=src,
            dst_ref=dst,
            send_sem=send_sem.at[index],
            recv_sem=recv_sem.at[index],
            device_id=device,
            device_id_type=MESH,
        )

    top = slice(planes - HMAX, planes)
    under = slice(planes, planes + HMAX)
    over = slice(planes + HMAX, planes + 2 * HMAX)

    def to_high():
        here = {"gy": high, "gz": mz}
        return [
            remote(height, halo_heights.at[0], 2, here),
            remote(vel_hbm.at[:, top, :], halo_u.at[:, 0:HMAX, :], 0, here),
            remote(send_s.at[1], halo_s.at[:, 0:HMAX, :], 1, here),
            remote(strips.at[0, top, :], halo_strips.at[1, under, :], 3, {"gy": high, "gz": left}),
            remote(strips.at[1, top, :], halo_strips.at[0, under, :], 4, {"gy": high, "gz": right}),
        ]

    def to_low():
        here = {"gy": low, "gz": mz}
        return [
            remote(height, halo_heights.at[1], 7, here),
            remote(vel_hbm.at[:, 0:HMAX, :], halo_u.at[:, HMAX : 2 * HMAX, :], 5, here),
            remote(send_s.at[0], halo_s.at[:, HMAX : 2 * HMAX, :], 6, here),
            remote(strips.at[0, 0:HMAX, :], halo_strips.at[1, over, :], 8, {"gy": low, "gz": left}),
            remote(strips.at[1, 0:HMAX, :], halo_strips.at[0, over, :], 9, {"gy": low, "gz": right}),
        ]

    def to_sides():
        return [
            remote(strips.at[0], halo_strips.at[1, 0:planes, :], 10, {"gy": my, "gz": left}),
            remote(strips.at[1], halo_strips.at[0, 0:planes, :], 11, {"gy": my, "gz": right}),
        ]

    def send_halo(which):
        @pl.when(has_high)
        def _():
            for copy in to_high()[which]:
                copy.start()

        @pl.when(has_low)
        def _():
            for copy in to_low()[which]:
                copy.start()

    send_halo(slice(0, 3))
    for copy in to_sides():
        copy.start()
    if rounds:
        tell(0)

    def notify(y):
        pl.semaphore_signal(
            passed, inc=1, device_id={"gy": y, "gz": mz}, device_id_type=MESH
        )

    pl.when(has_low)(lambda: notify(low))
    pl.when(has_high)(lambda: notify(high))

    def clear(side):
        span = slice(side * HMAX, (side + 1) * HMAX)
        halo_u[:, span, :] = jnp.zeros((3, HMAX, cells), jnp.float32)
        halo_s[:, span, :] = jnp.zeros((6, HMAX, cells), jnp.float32)
        halo_heights[side] = jnp.zeros(halo_heights.shape[1:], jnp.float32)
        start = planes + side * HMAX
        halo_strips[:, start : start + HMAX, :] = jnp.zeros((2, HMAX, LANES), jnp.float32)

    pl.when(jnp.logical_not(has_low))(lambda: clear(0))
    pl.when(jnp.logical_not(has_high))(lambda: clear(1))

    lax.fori_loop(ends // ROWS, planes // ROWS, own_block, 0)

    pl.semaphore_wait(passed, has_low.astype(jnp.int32) + has_high.astype(jnp.int32))
    send_halo(slice(3, 5))

    acc[...] = jnp.zeros_like(acc)
    width = 2 * LANES
    chunks = cells // width

    def put(ref, rows, start, x):
        hi, lo = halves(x)
        ref[rows, start : start + width] = hi
        ref[rows, cells + start : cells + start + width] = lo

    def band(weights, x):
        return jnp.dot(weights, x, preferred_element_type=jnp.float32)

    for f in range(FIELDS):
        for start in range(0, cells, width):
            lanes = slice(start, start + width)
            if 9 <= f < 15:
                s = strain[f - 9, :, lanes]
                x = band(weights_own, jnp.concatenate([s, s], axis=0))
            else:
                x = band(mask_own, pieces[f if f < 9 else f - 6, :, lanes])
            put(wall, slice(f * inner, (f + 1) * inner), start, x[:inner])
            rim[f, :, lanes] = x[inner:]

    def await_halo(which):
        @pl.when(has_low)
        def _():
            for copy in to_high()[which]:
                copy.wait_recv()

        @pl.when(has_high)
        def _():
            for copy in to_low()[which]:
                copy.wait_recv()

    def along(ref, rows, chunk):
        last = chunk == chunks - 1
        columns = []
        for base in (0, cells):
            first = base + chunk * width
            if last:
                columns.append(ref[rows, first : first + width])
                columns.append(ref[rows, base : base + LANES])
            else:
                columns.append(ref[rows, first : first + 3 * LANES])
        return jnp.dot(
            jnp.concatenate(columns, axis=1),
            (window_parted if last else window)[...],
            preferred_element_type=jnp.float32,
        )

    def contract(chunk, start, t):
        rows = slice(start, start + 8)
        lanes = slice(t * LANES, (t + 1) * LANES)
        q = norm[rows, :]

        def of(f):
            return filt[chunk, f, rows, lanes]

        tensor = [of(9 + c) for c in range(6)]
        rate = 4.0 * q * strain_rate(tensor)
        u = [of(c) for c in range(3)]
        qu = [q * x for x in u]
        sums = [[None, None], [None, None]]
        for k in range(6):
            leonard = of(3 + k) - qu[LEAD_INDEX[k]] * u[TAIL_INDEX[k]]
            model = of(15 + k) - rate * tensor[k]
            group = sums[0 if TENSOR_WEIGHTS[k] == 1.0 else 1]
            for at, term in enumerate((leonard * model, model * model)):
                group[at] = term if group[at] is None else group[at] + term
        for at in range(2):
            span = slice(at * LANES, (at + 1) * LANES)
            acc[rows, span] = acc[rows, span] + (sums[0][at] + 2.0 * sums[1][at])

    def jobs(chunk, first, stop):
        parts = [0] if chunk == chunks - 1 else [0, 1]
        return [(chunk, start, t) for start in range(first, stop, 8) for t in parts]

    step_fields = 3
    pending = []
    for chunk in range(chunks):
        share_of = -(-len(pending) // (FIELDS // step_fields))
        for f in range(0, FIELDS, step_fields):
            x = along(wall, slice(f * inner, (f + step_fields) * inner), chunk)
            filt[chunk, f : f + step_fields, 0:inner] = x.reshape(step_fields, inner, width)
            for job in pending[:share_of]:
                contract(*job)
            pending = pending[share_of:]
        pending = jobs(chunk, 0, inner)
    for job in pending:
        contract(*job)

    for r in range(1, rounds):
        hear(r - 1)
        tell(r)
    for copy in to_sides():
        copy.wait_recv()
    await_halo(slice(0, 3))

    strip_lane = lane_index(ROWS)
    group = strip_lane // (2 * NX)
    is_right = strip_lane % (2 * NX) < NX
    scale = jnp.where(group < 3, 2.0, jnp.where(group < 6, 4.0, 0.0))

    def form_strips(rows, into, hi_rows, lo_rows):
        h = upright_height[rows, :]
        from_left = halo_strips[0, rows, :]
        from_right = halo_strips[1, rows, :]
        a = jnp.where(is_right, from_right, from_left)
        b = jnp.where(is_right, pltpu.roll(from_right, LANES - NX, 1), pltpu.roll(from_left, NX, 1))
        b = jnp.where(group == 0, b, 0.0)
        ha = h * a
        hb = h * b
        total = scale * a * a
        for shift in (16, 32, 64):
            total = total + pltpu.roll(total, shift, 1)
        rate = jnp.sqrt(total)
        u2 = pltpu.roll(b, 6 * 16, 1) + pltpu.roll(b, 7 * 16, 1)
        mixed = pltpu.roll(ha * pltpu.roll(a, LANES - 16, 1), LANES - 16, 1)
        second = jnp.where(group < 6, rate * ha, ha * a)
        third = jnp.where(
            group < 5,
            hb + pltpu.roll(hb * b, 16, 1),
            jnp.where(group == 5, mixed, ha * u2),
        )
        for k, y in enumerate((ha, second, third)):
            hi, lo = halves(y)
            at = slice(k * LANES, (k + 1) * LANES)
            into[hi_rows, at] = hi
            into[lo_rows, at] = lo

    for start in range(0, planes, ROWS):
        rows = slice(start, start + ROWS)
        form_strips(rows, packed_pieces, rows, slice(planes + start, planes + start + ROWS))
    packed_out[...] = band(mask_own, packed_pieces[...])

    half = LANES // 2
    edge_lane = lane_index(8)
    joint = (edge_lane >= half - NX) & (edge_lane < half + NX)
    tail = slice(LANES, width)

    def add_edges(start):
        rows = slice(start, start + 8)
        edge = [streamwise4(packed_out[rows, k * LANES : (k + 1) * LANES]) for k in range(3)]
        for f in range(FIELDS):
            t, g = PACKED_AT[f]
            shift = (half - NX - 2 * NX * g) % LANES
            x = pltpu.roll(edge[t], shift, 1) if shift else edge[t]
            filt[chunks - 1, f, rows, tail] = filt[chunks - 1, f, rows, tail] + jnp.where(joint, x, 0.0)

    heights[1:2, 0:planes] = halo_heights[0]
    heights[2:3, 0:planes] = halo_heights[1]
    below_row = pltpu.roll(heights[1:2, :], HMAX, 1)
    above_row = pltpu.roll(heights[2:3, :], planes + HMAX, 1)
    lane_row = lax.broadcasted_iota(jnp.int32, (1, LANES), 1)
    row = jnp.where(
        lane_row < planes,
        heights[0:1, :],
        jnp.where(lane_row < planes + HMAX, below_row, above_row),
    )
    heights[0:1, :] = row
    rim_lane = lax.broadcasted_iota(jnp.int32, (ROWS, LANES), 1)
    rim_sub = lax.broadcasted_iota(jnp.int32, (ROWS, LANES), 0)
    upright_height[planes:all_planes, :] = jnp.broadcast_to(
        upright(0, rim_lane == rim_sub + planes), (ROWS, LANES)
    )
    rim_inside = inside[inner:planes, :]
    rim_weights = rim_inside * row
    norm[inner:planes, :] = jnp.broadcast_to(
        (1.0 / 16.0) / jnp.sum(rim_weights, axis=1, keepdims=True), (ROWS, LANES)
    )
    rim_mask = jnp.concatenate([rim_inside.astype(jnp.bfloat16)[:, planes:all_planes]] * 2, axis=1)
    rim_weights = jnp.concatenate(halves(rim_weights[:, planes:all_planes]), axis=1)

    rim_places = (slice(planes, all_planes), halo_pieces, slice(0, ROWS), slice(ROWS, 2 * ROWS))

    def rim_fields(first, stop):
        for f in range(first, stop):
            for start in range(0, cells, width):
                lanes = slice(start, start + width)
                if 9 <= f < 15:
                    s = halo_s[f - 9, :, lanes].astype(jnp.bfloat16)
                    x = band(rim_weights, jnp.concatenate([s, s], axis=0))
                else:
                    x = band(rim_mask, halo_pieces[f if f < 9 else f - 6, :, lanes])
                put(wall_rim, slice(f * ROWS, (f + 1) * ROWS), start, rim[f, :, lanes] + x)
        for chunk in range(chunks):
            x = along(wall_rim, slice(first * ROWS, stop * ROWS), chunk)
            filt[chunk, first:stop, inner:planes] = x.reshape(stop - first, ROWS, width)

    form_flow(lambda c, lanes: halo_u[c, :, lanes], *rim_places)
    form_rates(lambda c, lanes: halo_s[c, :, lanes], *rim_places)
    rim_fields(0, FIELDS)
    for start in range(0, inner, 8):
        add_edges(start)
        contract(chunks - 1, start, 1)
    for chunk in range(chunks):
        for job in jobs(chunk, inner, planes):
            contract(*job)

    await_halo(slice(3, 5))
    form_strips(
        slice(planes, all_planes), rim_packed, slice(0, ROWS), slice(ROWS, 2 * ROWS)
    )
    packed_out[inner:planes, :] = packed_out[inner:planes, :] + band(rim_mask, rim_packed[...])
    for start in range(inner, planes, 8):
        add_edges(start)
        contract(chunks - 1, start, 1)

    q = norm[...]
    scaled = jnp.concatenate([acc[:, 0:LANES] * (q * q), acc[:, LANES:width] * (q * q)], axis=1)
    pick_row = lax.broadcasted_iota(jnp.int32, (2, 2 * LANES), 0)
    pick_lane = lax.broadcasted_iota(jnp.int32, (2, 2 * LANES), 1)
    pick = jnp.where(pick_row == pick_lane // LANES, 1.0, 0.0)
    part[...] = jnp.zeros_like(part)
    part[:, 0:planes] = lax.dot_general(
        pick,
        scaled,
        (((1,), (1,)), ((), ())),
        precision=lax.Precision.HIGHEST,
        preferred_element_type=jnp.float32,
    )
    slots[pl.ds(mz, 1)] = part[...][None]

    def share(step, peer, slot, sem):
        return pltpu.make_async_remote_copy(
            src_ref=part,
            dst_ref=slots.at[slot],
            send_sem=part_send.at[step],
            recv_sem=part_recv.at[sem],
            device_id={"gy": my, "gz": peer},
            device_id_type=MESH,
        )

    if rounds:
        hear(rounds - 1)
    for step in range(1, n_z):
        peer = lax.rem(mz + step, n_z)
        share(step, peer, mz, step).start()
    for step in range(1, n_z):
        source = lax.rem(mz + n_z - step, n_z)
        share(step, source, source, step).wait_recv()
    total = jnp.zeros((2, LANES), jnp.float32)
    for k in range(n_z):
        total = total + slots[k]
    count = 1.0 * n_z * cells
    result = total[0:1] / count / (total[1:2] / count + 1e-6)
    inner_row = pltpu.roll(result, HMAX, 1)
    low_row = pltpu.roll(result, LANES - inner, 1)
    result = jnp.where(
        lane_row < HMAX, low_row, jnp.where(lane_row < planes - HMAX, inner_row, result)
    )
    out[...] = result[:, :planes]

    for step in range(1, n_z):
        peer = lax.rem(mz + step, n_z)
        share(step, peer, mz, step).wait_send()

    @pl.when(has_high)
    def _():
        for copy in to_high():
            copy.wait_send()

    @pl.when(has_low)
    def _():
        for copy in to_low():
            copy.wait_send()

    for copy in to_sides():
        copy.wait_send()


def local(velocity, strain, cell_height, stencil_reach):
    planes, cells = velocity.shape[1], velocity.shape[2]
    n_y = lax.axis_size("gy")
    n_z = lax.axis_size("gz")
    all_planes = planes + 2 * HMAX
    inner = planes - 2 * HMAX
    f32, bf16 = jnp.float32, jnp.bfloat16
    vmem = pl.BlockSpec(memory_space=pltpu.VMEM)
    result = pl.pallas_call(
        functools.partial(kernel, n_y, n_z),
        out_shape=jax.ShapeDtypeStruct((1, planes), f32),
        in_specs=[pl.BlockSpec(memory_space=pltpu.HBM)] * 4,
        out_specs=vmem,
        scratch_shapes=[
            pltpu.VMEM((3, planes, cells), f32),
            pltpu.VMEM((6, planes, cells), bf16),
            pltpu.VMEM((1, planes), f32),
            pltpu.VMEM((2, planes), jnp.int32),
            pltpu.VMEM((FIELDS - 6, 2 * planes, cells), bf16),
            pltpu.VMEM((FIELDS - 6, 2 * ROWS, cells), bf16),
            pltpu.VMEM((FIELDS * inner, 2 * cells), bf16),
            pltpu.VMEM((FIELDS * ROWS, 2 * cells), bf16),
            pltpu.VMEM((FIELDS, ROWS, cells), f32),
            pltpu.VMEM((6 * LANES, 2 * LANES), bf16),
            pltpu.VMEM((6 * LANES, 2 * LANES), bf16),
            pltpu.VMEM((2 * planes, 3 * LANES), bf16),
            pltpu.VMEM((2 * ROWS, 3 * LANES), bf16),
            pltpu.VMEM((planes, 3 * LANES), f32),
            pltpu.VMEM((cells // (2 * LANES), FIELDS, planes, 2 * LANES), f32),
            pltpu.VMEM((3, 2 * HMAX, cells), f32),
            pltpu.VMEM((6, 2 * HMAX, cells), f32),
            pltpu.VMEM((2, 6, HMAX, cells), f32),
            pltpu.VMEM((2, planes, LANES), f32),
            pltpu.VMEM((2, all_planes, LANES), f32),
            pltpu.VMEM((8, LANES), f32),
            pltpu.VMEM((2, 1, planes), f32),
            pltpu.VMEM((all_planes, LANES), f32),
            pltpu.VMEM((planes, LANES), f32),
            pltpu.VMEM((planes, 2 * LANES), f32),
            pltpu.VMEM((2, LANES), f32),
            pltpu.VMEM((n_z, 2, LANES), f32),
            pltpu.SemaphoreType.DMA((12,)),
            pltpu.SemaphoreType.DMA((12,)),
            pltpu.SemaphoreType.DMA((n_z,)),
            pltpu.SemaphoreType.DMA((n_z,)),
            pltpu.SemaphoreType.DMA((8,)),
            pltpu.SemaphoreType.REGULAR((max((n_z // 2 - 1).bit_length(), 1),)),
            pltpu.SemaphoreType.REGULAR,
            pltpu.VMEM((planes, LANES), f32),
        ],
        compiler_params=pltpu.CompilerParams(
            collective_id=0, has_side_effects=True, vmem_limit_bytes=67043328 - 10490000
        ),
    )(velocity, strain, cell_height.reshape(1, planes), stencil_reach)
    return result.reshape(planes)


def solution(mesh):
    in_specs = (P(None, "gy", "gz"), P(None, "gy", "gz"), P("gy"), P(None, "gy"))
    return jax.shard_map(local, mesh=mesh, in_specs=in_specs, out_specs=P("gy"), check_vma=False)
```

```python
import functools

import jax
import jax.numpy as jnp
from jax import lax
from jax.experimental import pallas as pl
from jax.experimental.pallas import tpu as pltpu
from jax.sharding import PartitionSpec as P

NX = 8
HMAX = 8
LANES = 128
ROWS = 16

LEAD_INDEX = (0, 1, 2, 0, 0, 1)
TAIL_INDEX = (0, 1, 2, 1, 2, 2)
TENSOR_WEIGHTS = (1.0, 1.0, 1.0, 2.0, 2.0, 2.0)
FIELDS = 21
PACKED_AT = (
    [(0, 6), (0, 7), (2, 0)]
    + [(1, 6), (1, 7), (2, 1), (2, 5), (2, 6), (2, 7)]
    + [(0, c) for c in range(6)]
    + [(1, c) for c in range(6)]
)
MESH = pl.DeviceIdType.MESH


def strain_rate(t):
    squares = 2.0 * (t[0] * t[0] + t[1] * t[1] + t[2] * t[2])
    return jnp.sqrt(squares + 4.0 * (t[3] * t[3] + t[4] * t[4] + t[5] * t[5]))


def lane_index(rows):
    return lax.broadcasted_iota(jnp.int32, (rows, LANES), 1)


def streamwise4(x):
    position = lane_index(x.shape[0]) % NX
    behind = jnp.where(
        position == 0, pltpu.roll(x, LANES + 1 - NX, 1), pltpu.roll(x, 1, 1)
    )
    ahead = jnp.where(
        position == NX - 1, pltpu.roll(x, NX - 1, 1), pltpu.roll(x, LANES - 1, 1)
    )
    return behind + ahead + (x + x)


def horizontal(window, parted):
    shape = (3 * LANES, 2 * LANES)
    source = lax.broadcasted_iota(jnp.int32, shape, 0)
    target = lax.broadcasted_iota(jnp.int32, shape, 1) + LANES // 2
    cells_apart = jnp.abs(source // NX - target // NX)
    along = (source - target) & (NX - 1)
    span = jnp.where(cells_apart == 0, 2.0, jnp.where(cells_apart == 1, 1.0, 0.0))
    stream = jnp.where(along == 0, 2.0, jnp.where((along == 1) | (along == NX - 1), 1.0, 0.0))
    both = span * stream
    if parted:
        both = jnp.where((source < 2 * LANES) == (target < 2 * LANES), both, 0.0)
    both = both.astype(jnp.bfloat16)
    window[0 : 3 * LANES, :] = both
    window[3 * LANES : 6 * LANES, :] = both


def halves(x):
    high = x.astype(jnp.bfloat16)
    return high, (x - high.astype(jnp.float32)).astype(jnp.bfloat16)


def kernel(
    n_y,
    n_z,
    vel_hbm,
    strain_hbm,
    height_hbm,
    reach_hbm,
    out,
    vel,
    strain,
    height,
    reach,
    pieces,
    halo_pieces,
    wall,
    wall_rim,
    rim,
    window,
    window_parted,
    packed_pieces,
    rim_packed,
    packed_out,
    filt,
    halo_u,
    halo_s,
    send_s,
    strips,
    halo_strips,
    heights,
    halo_heights,
    upright_height,
    norm,
    acc,
    part,
    slots,
    send_sem,
    recv_sem,
    part_send,
    part_recv,
    load_sem,
    known,
    passed,
    inside,
):
    planes, cells = vel.shape[1], vel.shape[2]
    all_planes = planes + 2 * HMAX
    inner = planes - 2 * HMAX
    bottom = slice(0, ROWS)
    middle = slice(ROWS, planes - ROWS)
    summit = slice(planes - ROWS, planes)
    whole = slice(0, planes)
    first_tile = slice(0, LANES)
    last_tile = slice(cells - LANES, cells)
    between = slice(LANES, cells - LANES)
    loads = [
        pltpu.make_async_copy(src.at[:, rows, lanes], dst.at[:, rows, lanes], load_sem.at[k])
        for k, (src, dst, rows, lanes) in enumerate(
            [
                (strain_hbm, strain, whole, first_tile),
                (strain_hbm, strain, whole, last_tile),
                (vel_hbm, vel, whole, first_tile),
                (vel_hbm, vel, whole, last_tile),
                (strain_hbm, strain, bottom, between),
                (strain_hbm, strain, summit, between),
                (strain_hbm, strain, middle, between),
                (vel_hbm, vel, whole, between),
            ]
        )
    ]
    tables = [
        pltpu.make_async_copy(height_hbm, height, load_sem.at[8]),
        pltpu.make_async_copy(reach_hbm, reach, load_sem.at[9]),
    ]
    for copy in tables:
        copy.start()
    for copy in loads:
        copy.start()
    tiles = cells // LANES
    my = lax.axis_index("gy")
    mz = lax.axis_index("gz")
    right = lax.rem(mz + 1, n_z)
    left = lax.rem(mz + n_z - 1, n_z)
    has_low = my > 0
    has_high = my < n_y - 1
    low = my - 1
    high = my + 1

    barrier = pltpu.get_barrier_semaphore()

    def greet(device):
        pl.semaphore_signal(barrier, inc=1, device_id=device, device_id_type=MESH)

    greet({"gy": my, "gz": left})
    greet({"gy": my, "gz": right})
    pl.when(has_low)(lambda: greet({"gy": low, "gz": mz}))
    pl.when(has_high)(lambda: greet({"gy": high, "gz": mz}))

    horizontal(window, False)
    horizontal(window_parted, True)

    def pack(i, carry):
        rows = pl.ds(pl.multiple_of(i * ROWS, ROWS), ROWS)
        lane = lane_index(ROWS)
        first = jnp.zeros((ROWS, LANES), jnp.float32)
        last = first
        for g in range(9):
            def tile(start):
                if g < 6:
                    return strain[g, rows, start : start + LANES].astype(jnp.float32)
                return vel[g - 6, rows, start : start + LANES]

            a = tile(0)
            b = tile(cells - LANES)
            to_first = 2 * g * NX if g < 8 else NX
            to_last = (2 * g + 1) * NX if g < 8 else 0
            a = pltpu.roll(a, to_first, 1) if to_first else a
            move = (to_last + NX) % LANES
            b = pltpu.roll(b, move, 1) if move else b
            first = jnp.where((lane >= to_first) & (lane < to_first + NX), a, first)
            last = jnp.where((lane >= to_last) & (lane < to_last + NX), b, last)
        strips[0, rows, :] = first
        strips[1, rows, :] = last
        return carry


    def emit_to(into, hi_rows, lo_rows, lanes):
        def emit(f, x):
            hi, lo = halves(x)
            into[f, hi_rows, lanes] = hi
            into[f, lo_rows, lanes] = lo

        return emit

    def form_rates(load_s, height_rows, into, hi_rows, lo_rows):
        h = upright_height[height_rows, :]
        for t in range(tiles):
            lanes = slice(t * LANES, (t + 1) * LANES)
            emit = emit_to(into, hi_rows, lo_rows, lanes)
            s = [load_s(c, lanes) for c in range(6)]
            rate = h * strain_rate(s)
            for c in range(6):
                emit(9 + c, rate * s[c])

    def form_flow(load_u, height_rows, into, hi_rows, lo_rows):
        h = upright_height[height_rows, :]
        for t in range(tiles):
            lanes = slice(t * LANES, (t + 1) * LANES)
            emit = emit_to(into, hi_rows, lo_rows, lanes)
            u = [load_u(c, lanes) for c in range(3)]
            hu = [h * x for x in u]
            for c in range(3):
                emit(c, hu[c])
            for k in range(6):
                emit(3 + k, hu[LEAD_INDEX[k]] * u[TAIL_INDEX[k]])

    def own_block(i, carry):
        start = pl.multiple_of(i * ROWS, ROWS)
        rows = pl.ds(start, ROWS)
        places = (rows, pieces, rows, pl.ds(start + planes, ROWS))
        form_rates(lambda c, lanes: strain[c, rows, lanes].astype(jnp.float32), *places)
        form_flow(lambda c, lanes: vel[c, rows, lanes], *places)
        return carry

    for copy in loads[:4]:
        copy.wait()
    lax.fori_loop(0, planes // ROWS, pack, 0)
    for copy in loads[4:6]:
        copy.wait()
    for c in range(6):
        send_s[0, c] = strain[c, 0:ROWS, :].astype(jnp.float32)[0:HMAX]
        send_s[1, c] = strain[c, planes - ROWS : planes, :].astype(jnp.float32)[HMAX:ROWS]

    for copy in tables:
        copy.wait()

    partners = 2 + has_low.astype(jnp.int32) + has_high.astype(jnp.int32)
    pl.semaphore_wait(barrier, partners)

    def tell(r):
        for z in (lax.rem(mz + 2**r, n_z), lax.rem(mz + n_z - 2**r, n_z)):
            pl.semaphore_signal(
                known.at[r], inc=1, device_id={"gy": my, "gz": z}, device_id_type=MESH
            )

    def hear(r):
        pl.semaphore_wait(known.at[r], 2)

    rounds = max((n_z // 2 - 1).bit_length(), 0)

    def remote(src, dst, index, device):
        return pltpu.make_async_remote_copy(
            src_ref=src,
            dst_ref=dst,
            send_sem=send_sem.at[index],
            recv_sem=recv_sem.at[index],
            device_id=device,
            device_id_type=MESH,
        )

    top = slice(planes - HMAX, planes)
    under = slice(planes, planes + HMAX)
    over = slice(planes + HMAX, planes + 2 * HMAX)

    def to_high():
        here = {"gy": high, "gz": mz}
        return [
            remote(height, halo_heights.at[0], 2, here),
            remote(vel_hbm.at[:, top, :], halo_u.at[:, 0:HMAX, :], 0, here),
            remote(send_s.at[1], halo_s.at[:, 0:HMAX, :], 1, here),
            remote(strips.at[0, top, :], halo_strips.at[1, under, :], 3, {"gy": high, "gz": left}),
            remote(strips.at[1, top, :], halo_strips.at[0, under, :], 4, {"gy": high, "gz": right}),
        ]

    def to_low():
        here = {"gy": low, "gz": mz}
        return [
            remote(height, halo_heights.at[1], 7, here),
            remote(vel_hbm.at[:, 0:HMAX, :], halo_u.at[:, HMAX : 2 * HMAX, :], 5, here),
            remote(send_s.at[0], halo_s.at[:, HMAX : 2 * HMAX, :], 6, here),
            remote(strips.at[0, 0:HMAX, :], halo_strips.at[1, over, :], 8, {"gy": low, "gz": left}),
            remote(strips.at[1, 0:HMAX, :], halo_strips.at[0, over, :], 9, {"gy": low, "gz": right}),
        ]

    def to_sides():
        return [
            remote(strips.at[0], halo_strips.at[1, 0:planes, :], 10, {"gy": my, "gz": left}),
            remote(strips.at[1], halo_strips.at[0, 0:planes, :], 11, {"gy": my, "gz": right}),
        ]

    def send_halo(which):
        @pl.when(has_high)
        def _():
            for copy in to_high()[which]:
                copy.start()

        @pl.when(has_low)
        def _():
            for copy in to_low()[which]:
                copy.start()

    send_halo(slice(0, 3))
    for copy in to_sides():
        copy.start()
    if rounds:
        tell(0)

    def notify(y):
        pl.semaphore_signal(
            passed, inc=1, device_id={"gy": y, "gz": mz}, device_id_type=MESH
        )

    pl.when(has_low)(lambda: notify(low))
    pl.when(has_high)(lambda: notify(high))

    def clear(side):
        span = slice(side * HMAX, (side + 1) * HMAX)
        halo_u[:, span, :] = jnp.zeros((3, HMAX, cells), jnp.float32)
        halo_s[:, span, :] = jnp.zeros((6, HMAX, cells), jnp.float32)
        halo_heights[side] = jnp.zeros(halo_heights.shape[1:], jnp.float32)
        start = planes + side * HMAX
        halo_strips[:, start : start + HMAX, :] = jnp.zeros((2, HMAX, LANES), jnp.float32)

    pl.when(jnp.logical_not(has_low))(lambda: clear(0))
    pl.when(jnp.logical_not(has_high))(lambda: clear(1))

    heights[...] = jnp.zeros_like(heights)
    heights[0:1, 0:planes] = height[...]
    heights[3:5, 0:planes] = reach[...].astype(jnp.float32)
    lane = lax.broadcasted_iota(jnp.int32, (planes, LANES), 1)
    sub = lax.broadcasted_iota(jnp.int32, (planes, LANES), 0)
    own = jnp.where(sub < inner, sub + HMAX, jnp.where(sub < inner + HMAX, sub - inner, sub))
    offset = my * planes
    column = offset + jnp.where(
        lane < planes, lane, jnp.where(lane < planes + HMAX, lane - planes - HMAX, lane - HMAX)
    )

    def upright(k, at):
        rows = at.shape[0]
        spread = jnp.where(at, jnp.broadcast_to(heights[k : k + 1, :], (rows, LANES)), 0.0)
        return jnp.sum(spread, axis=1, keepdims=True)

    picked = lane == own
    plane = offset + own
    lowest = jnp.maximum(plane - upright(3, picked).astype(jnp.int32), 0)
    highest = jnp.minimum(plane + upright(4, picked).astype(jnp.int32), n_y * planes - 1)
    allowed = (column >= lowest) & (column <= highest) & (lane < all_planes)
    within = jnp.where(allowed, 1.0, 0.0)
    inside[...] = within
    own_row = heights[0:1, :]
    upright_height[0:planes, :] = jnp.broadcast_to(upright(0, lane == sub), (planes, LANES))
    weights = within * own_row
    total = jnp.sum(weights[0:inner], axis=1, keepdims=True)
    norm[0:inner, :] = jnp.broadcast_to((1.0 / 16.0) / total, (inner, LANES))
    mask = within.astype(jnp.bfloat16)
    mask_own = jnp.concatenate([mask[:, :planes]] * 2, axis=1)
    weights_own = jnp.concatenate(halves(weights[:, :planes]), axis=1)

    for copy in loads[6:]:
        copy.wait()
    blocks = planes // ROWS
    lax.fori_loop(0, blocks - 2, own_block, 0)

    pl.semaphore_wait(passed, has_low.astype(jnp.int32) + has_high.astype(jnp.int32))
    send_halo(slice(3, 5))
    lax.fori_loop(blocks - 2, blocks, own_block, 0)

    acc[...] = jnp.zeros_like(acc)
    width = 2 * LANES
    chunks = cells // width

    def put(ref, rows, start, x):
        hi, lo = halves(x)
        ref[rows, start : start + width] = hi
        ref[rows, cells + start : cells + start + width] = lo

    def band(weights, x):
        return jnp.dot(weights, x, preferred_element_type=jnp.float32)

    for f in range(FIELDS):
        for start in range(0, cells, width):
            lanes = slice(start, start + width)
            if 9 <= f < 15:
                s = strain[f - 9, :, lanes]
                x = band(weights_own, jnp.concatenate([s, s], axis=0))
            else:
                x = band(mask_own, pieces[f if f < 9 else f - 6, :, lanes])
            put(wall, slice(f * inner, (f + 1) * inner), start, x[:inner])
            rim[f, :, lanes] = x[inner:]

    def await_halo(which):
        @pl.when(has_low)
        def _():
            for copy in to_high()[which]:
                copy.wait_recv()

        @pl.when(has_high)
        def _():
            for copy in to_low()[which]:
                copy.wait_recv()

    def along(ref, rows, chunk):
        last = chunk == chunks - 1
        columns = []
        for base in (0, cells):
            first = base + chunk * width
            if last:
                columns.append(ref[rows, first : first + width])
                columns.append(ref[rows, base : base + LANES])
            else:
                columns.append(ref[rows, first : first + 3 * LANES])
        return jnp.dot(
            jnp.concatenate(columns, axis=1),
            (window_parted if last else window)[...],
            preferred_element_type=jnp.float32,
        )

    def contract(chunk, start, t):
        rows = slice(start, start + 8)
        lanes = slice(t * LANES, (t + 1) * LANES)
        q = norm[rows, :]

        def of(f):
            return filt[chunk, f, rows, lanes]

        tensor = [of(9 + c) for c in range(6)]
        rate = 4.0 * q * strain_rate(tensor)
        u = [of(c) for c in range(3)]
        qu = [q * x for x in u]
        sums = [[None, None], [None, None]]
        for k in range(6):
            leonard = of(3 + k) - qu[LEAD_INDEX[k]] * u[TAIL_INDEX[k]]
            model = of(15 + k) - rate * tensor[k]
            group = sums[0 if TENSOR_WEIGHTS[k] == 1.0 else 1]
            for at, term in enumerate((leonard * model, model * model)):
                group[at] = term if group[at] is None else group[at] + term
        for at in range(2):
            span = slice(at * LANES, (at + 1) * LANES)
            acc[rows, span] = acc[rows, span] + (sums[0][at] + 2.0 * sums[1][at])

    def jobs(chunk, first, stop):
        parts = [0] if chunk == chunks - 1 else [0, 1]
        return [(chunk, start, t) for start in range(first, stop, 8) for t in parts]

    step_fields = 3
    pending = []
    for chunk in range(chunks):
        share_of = -(-len(pending) // (FIELDS // step_fields))
        for f in range(0, FIELDS, step_fields):
            x = along(wall, slice(f * inner, (f + step_fields) * inner), chunk)
            filt[chunk, f : f + step_fields, 0:inner] = x.reshape(step_fields, inner, width)
            for job in pending[:share_of]:
                contract(*job)
            pending = pending[share_of:]
        pending = jobs(chunk, 0, inner)
    for job in pending:
        contract(*job)

    for r in range(1, rounds):
        hear(r - 1)
        tell(r)
    for copy in to_sides():
        copy.wait_recv()
    await_halo(slice(0, 3))

    strip_lane = lane_index(ROWS)
    group = strip_lane // (2 * NX)
    is_right = strip_lane % (2 * NX) < NX
    scale = jnp.where(group < 3, 2.0, jnp.where(group < 6, 4.0, 0.0))

    def form_strips(rows, into, hi_rows, lo_rows):
        h = upright_height[rows, :]
        from_left = halo_strips[0, rows, :]
        from_right = halo_strips[1, rows, :]
        a = jnp.where(is_right, from_right, from_left)
        b = jnp.where(is_right, pltpu.roll(from_right, LANES - NX, 1), pltpu.roll(from_left, NX, 1))
        b = jnp.where(group == 0, b, 0.0)
        ha = h * a
        hb = h * b
        total = scale * a * a
        for shift in (16, 32, 64):
            total = total + pltpu.roll(total, shift, 1)
        rate = jnp.sqrt(total)
        u2 = pltpu.roll(b, 6 * 16, 1) + pltpu.roll(b, 7 * 16, 1)
        mixed = pltpu.roll(ha * pltpu.roll(a, LANES - 16, 1), LANES - 16, 1)
        second = jnp.where(group < 6, rate * ha, ha * a)
        third = jnp.where(
            group < 5,
            hb + pltpu.roll(hb * b, 16, 1),
            jnp.where(group == 5, mixed, ha * u2),
        )
        for k, y in enumerate((ha, second, third)):
            hi, lo = halves(y)
            at = slice(k * LANES, (k + 1) * LANES)
            into[hi_rows, at] = hi
            into[lo_rows, at] = lo

    for start in range(0, planes, ROWS):
        rows = slice(start, start + ROWS)
        form_strips(rows, packed_pieces, rows, slice(planes + start, planes + start + ROWS))
    packed_out[...] = band(mask_own, packed_pieces[...])

    half = LANES // 2
    edge_lane = lane_index(8)
    joint = (edge_lane >= half - NX) & (edge_lane < half + NX)
    tail = slice(LANES, width)

    def add_edges(start):
        rows = slice(start, start + 8)
        edge = [streamwise4(packed_out[rows, k * LANES : (k + 1) * LANES]) for k in range(3)]
        for f in range(FIELDS):
            t, g = PACKED_AT[f]
            shift = (half - NX - 2 * NX * g) % LANES
            x = pltpu.roll(edge[t], shift, 1) if shift else edge[t]
            filt[chunks - 1, f, rows, tail] = filt[chunks - 1, f, rows, tail] + jnp.where(joint, x, 0.0)

    heights[1:2, 0:planes] = halo_heights[0]
    heights[2:3, 0:planes] = halo_heights[1]
    below_row = pltpu.roll(heights[1:2, :], HMAX, 1)
    above_row = pltpu.roll(heights[2:3, :], planes + HMAX, 1)
    lane_row = lax.broadcasted_iota(jnp.int32, (1, LANES), 1)
    row = jnp.where(
        lane_row < planes,
        heights[0:1, :],
        jnp.where(lane_row < planes + HMAX, below_row, above_row),
    )
    heights[0:1, :] = row
    rim_lane = lax.broadcasted_iota(jnp.int32, (ROWS, LANES), 1)
    rim_sub = lax.broadcasted_iota(jnp.int32, (ROWS, LANES), 0)
    upright_height[planes:all_planes, :] = jnp.broadcast_to(
        upright(0, rim_lane == rim_sub + planes), (ROWS, LANES)
    )
    rim_inside = inside[inner:planes, :]
    rim_weights = rim_inside * row
    norm[inner:planes, :] = jnp.broadcast_to(
        (1.0 / 16.0) / jnp.sum(rim_weights, axis=1, keepdims=True), (ROWS, LANES)
    )
    rim_mask = jnp.concatenate([rim_inside.astype(jnp.bfloat16)[:, planes:all_planes]] * 2, axis=1)
    rim_weights = jnp.concatenate(halves(rim_weights[:, planes:all_planes]), axis=1)

    rim_places = (slice(planes, all_planes), halo_pieces, slice(0, ROWS), slice(ROWS, 2 * ROWS))

    starts = list(range(0, inner, 8))

    def edge_step():
        if starts:
            start = starts.pop(0)
            add_edges(start)
            contract(chunks - 1, start, 1)

    def rim_fields(first, stop):
        for f in range(first, stop):
            if f % 2:
                edge_step()
            for start in range(0, cells, width):
                lanes = slice(start, start + width)
                if 9 <= f < 15:
                    s = halo_s[f - 9, :, lanes].astype(jnp.bfloat16)
                    x = band(rim_weights, jnp.concatenate([s, s], axis=0))
                else:
                    x = band(rim_mask, halo_pieces[f if f < 9 else f - 6, :, lanes])
                put(wall_rim, slice(f * ROWS, (f + 1) * ROWS), start, rim[f, :, lanes] + x)
        for chunk in range(chunks):
            x = along(wall_rim, slice(first * ROWS, stop * ROWS), chunk)
            filt[chunk, first:stop, inner:planes] = x.reshape(stop - first, ROWS, width)

    form_flow(lambda c, lanes: halo_u[c, :, lanes], *rim_places)
    form_rates(lambda c, lanes: halo_s[c, :, lanes], *rim_places)
    rim_fields(0, FIELDS)
    while starts:
        edge_step()
    for chunk in range(chunks):
        for job in jobs(chunk, inner, planes):
            contract(*job)

    await_halo(slice(3, 5))
    form_strips(
        slice(planes, all_planes), rim_packed, slice(0, ROWS), slice(ROWS, 2 * ROWS)
    )
    packed_out[inner:planes, :] = packed_out[inner:planes, :] + band(rim_mask, rim_packed[...])
    for start in range(inner, planes, 8):
        add_edges(start)
        contract(chunks - 1, start, 1)

    q = norm[...]
    scaled = jnp.concatenate([acc[:, 0:LANES] * (q * q), acc[:, LANES:width] * (q * q)], axis=1)
    pick_row = lax.broadcasted_iota(jnp.int32, (2, 2 * LANES), 0)
    pick_lane = lax.broadcasted_iota(jnp.int32, (2, 2 * LANES), 1)
    pick = jnp.where(pick_row == pick_lane // LANES, 1.0, 0.0)
    part[...] = jnp.zeros_like(part)
    part[:, 0:planes] = lax.dot_general(
        pick,
        scaled,
        (((1,), (1,)), ((), ())),
        precision=lax.Precision.HIGHEST,
        preferred_element_type=jnp.float32,
    )
    slots[pl.ds(mz, 1)] = part[...][None]

    def share(step, peer, slot, sem):
        return pltpu.make_async_remote_copy(
            src_ref=part,
            dst_ref=slots.at[slot],
            send_sem=part_send.at[step],
            recv_sem=part_recv.at[sem],
            device_id={"gy": my, "gz": peer},
            device_id_type=MESH,
        )

    if rounds:
        hear(rounds - 1)
    for step in range(1, n_z):
        peer = lax.rem(mz + step, n_z)
        share(step, peer, mz, step).start()
    for step in range(1, n_z):
        source = lax.rem(mz + n_z - step, n_z)
        share(step, source, source, step).wait_recv()
    total = jnp.zeros((2, LANES), jnp.float32)
    for k in range(n_z):
        total = total + slots[k]
    count = 1.0 * n_z * cells
    result = total[0:1] / count / (total[1:2] / count + 1e-6)
    inner_row = pltpu.roll(result, HMAX, 1)
    low_row = pltpu.roll(result, LANES - inner, 1)
    result = jnp.where(
        lane_row < HMAX, low_row, jnp.where(lane_row < planes - HMAX, inner_row, result)
    )
    out[...] = result[:, :planes]

    for step in range(1, n_z):
        peer = lax.rem(mz + step, n_z)
        share(step, peer, mz, step).wait_send()

    @pl.when(has_high)
    def _():
        for copy in to_high():
            copy.wait_send()

    @pl.when(has_low)
    def _():
        for copy in to_low():
            copy.wait_send()

    for copy in to_sides():
        copy.wait_send()


def local(velocity, strain, cell_height, stencil_reach):
    planes, cells = velocity.shape[1], velocity.shape[2]
    n_y = lax.axis_size("gy")
    n_z = lax.axis_size("gz")
    all_planes = planes + 2 * HMAX
    inner = planes - 2 * HMAX
    f32, bf16 = jnp.float32, jnp.bfloat16
    vmem = pl.BlockSpec(memory_space=pltpu.VMEM)
    result = pl.pallas_call(
        functools.partial(kernel, n_y, n_z),
        out_shape=jax.ShapeDtypeStruct((1, planes), f32),
        in_specs=[pl.BlockSpec(memory_space=pltpu.HBM)] * 4,
        out_specs=vmem,
        scratch_shapes=[
            pltpu.VMEM((3, planes, cells), f32),
            pltpu.VMEM((6, planes, cells), bf16),
            pltpu.VMEM((1, planes), f32),
            pltpu.VMEM((2, planes), jnp.int32),
            pltpu.VMEM((FIELDS - 6, 2 * planes, cells), bf16),
            pltpu.VMEM((FIELDS - 6, 2 * ROWS, cells), bf16),
            pltpu.VMEM((FIELDS * inner, 2 * cells), bf16),
            pltpu.VMEM((FIELDS * ROWS, 2 * cells), bf16),
            pltpu.VMEM((FIELDS, ROWS, cells), f32),
            pltpu.VMEM((6 * LANES, 2 * LANES), bf16),
            pltpu.VMEM((6 * LANES, 2 * LANES), bf16),
            pltpu.VMEM((2 * planes, 3 * LANES), bf16),
            pltpu.VMEM((2 * ROWS, 3 * LANES), bf16),
            pltpu.VMEM((planes, 3 * LANES), f32),
            pltpu.VMEM((cells // (2 * LANES), FIELDS, planes, 2 * LANES), f32),
            pltpu.VMEM((3, 2 * HMAX, cells), f32),
            pltpu.VMEM((6, 2 * HMAX, cells), f32),
            pltpu.VMEM((2, 6, HMAX, cells), f32),
            pltpu.VMEM((2, planes, LANES), f32),
            pltpu.VMEM((2, all_planes, LANES), f32),
            pltpu.VMEM((8, LANES), f32),
            pltpu.VMEM((2, 1, planes), f32),
            pltpu.VMEM((all_planes, LANES), f32),
            pltpu.VMEM((planes, LANES), f32),
            pltpu.VMEM((planes, 2 * LANES), f32),
            pltpu.VMEM((2, LANES), f32),
            pltpu.VMEM((n_z, 2, LANES), f32),
            pltpu.SemaphoreType.DMA((12,)),
            pltpu.SemaphoreType.DMA((12,)),
            pltpu.SemaphoreType.DMA((n_z,)),
            pltpu.SemaphoreType.DMA((n_z,)),
            pltpu.SemaphoreType.DMA((10,)),
            pltpu.SemaphoreType.REGULAR((max((n_z // 2 - 1).bit_length(), 1),)),
            pltpu.SemaphoreType.REGULAR,
            pltpu.VMEM((planes, LANES), f32),
        ],
        compiler_params=pltpu.CompilerParams(
            collective_id=0, has_side_effects=True, vmem_limit_bytes=67043328 - 10490000
        ),
    )(velocity, strain, cell_height.reshape(1, planes), stencil_reach)
    return result.reshape(planes)


def solution(mesh):
    in_specs = (P(None, "gy", "gz"), P(None, "gy", "gz"), P("gy"), P(None, "gy"))
    return jax.shard_map(local, mesh=mesh, in_specs=in_specs, out_specs=P("gy"), check_vma=False)
```
